32 devices in a mesh: aux: 32 (over z, y, x, core).
Axes of the slice: x: 2, y: 2, z: 4, core: 2. Of those that a mesh axis runs over, the one named last changes fastest.
Arguments:
- state: float32 [32, 2, 256, 256], P('aux'), may hold values from -6 to 6
- h_static: float32 [2, 256, 256], replicated, may hold values from -0.375 to 0.375
- drive_op: float32 [2, 256, 256], replicated, may hold values from -0.375 to 0.375
- couple: float32 [3, 256, 256], replicated, may hold values from -0.375 to 0.375
- bath_coef: float32 [2, 3], replicated, may hold values from -2 to 2
- damping: float32 [3], replicated, may hold values from 0.3 to 3
- occupation: int32 [32, 3], P('aux'), may hold values from 1 to 3
- raise_nbr: int32 [32, 3], P('aux'), may hold values from -1 to 31, as said below
- lower_nbr: int32 [32, 3], P('aux'), may hold values from -1 to 31, as said below
Outputs:
- new_state: float32 [32, 2, 256, 256], P('aux')
The draws below stay inside these ranges and needn't reach their ends.
Inputs may be any that keep to these rules, and one draw needn't show every extreme that they name: `raise_nbr`: each entry is -1 or the index of an auxiliary matrix held on a device 1 to 2 after its own holder (auxiliary a is held by device a); the first mode's entry is -1 only on the last 2 devices. `lower_nbr`: each entry is -1 or the index of an auxiliary matrix held on a device 1 to 2 before its own holder (auxiliary a is held by device a); the first mode's entry is -1 only on the first 2 devices.
All inputs are finite; a program needn't handle non-finite values.
Results may differ from the reference program's by a relative error of at most 0.0003.
Values sent between devices are 32-bit elements; how exact they have to be, the bound alone decides.
No kernel may reach another device: no remote copies, remote signals or barrier semaphores. Data moves between devices by JAX's collectives and lax.ppermute only.
A program may use at most 64 MiB of HBM per device.

```python
import math
import jax
import jax.numpy as jnp
from jax import lax

M = 256
MODES = 3
SPAN = 2
AUX_DEV = 1
AUXILIARIES = 32


def neighbour_list(key, sign):
    key_off, key_rot, key_slot, key_keep = jax.random.split(key, 4)
    holder = jnp.arange(AUXILIARIES, dtype=jnp.int32) // AUX_DEV
    offsets = jax.random.randint(key_off, (AUXILIARIES, MODES), 1, SPAN + 1)
    rotation = jax.random.randint(key_rot, (), 0, SPAN)
    first_col = 1 + (holder + rotation) % SPAN
    offsets = offsets.at[:, 0].set(first_col)
    slots = jax.random.randint(key_slot, (AUXILIARIES, MODES), 0, AUX_DEV)
    keeper = jax.random.randint(key_keep, (AUXILIARIES, MODES), 0, 8) > 0
    keeper = keeper.at[:, 0].set(True)
    device_of = holder[:, None] + sign * offsets
    target = device_of * AUX_DEV + slots
    usable = keeper & (device_of >= 0) & (device_of < AUXILIARIES // AUX_DEV)
    return jnp.where(usable, target, -1).astype(jnp.int32)


def draw_raise_nbr(key, part):
    return neighbour_list(jax.random.fold_in(key, 11), 1)


def draw_lower_nbr(key, part):
    return neighbour_list(jax.random.fold_in(key, 23), -1)


def place_ends(drawn, key, low, top_value):
    index_at = [jax.random.randint(jax.random.fold_in(key, axis), (), 0, length) for axis, length in enumerate(drawn.shape)]
    longest = drawn.shape.index(max(drawn.shape))
    beside = index_at[:longest] + [(index_at[longest] + 1) % drawn.shape[longest]] + index_at[longest + 1:]
    return drawn.at[tuple(index_at)].set(low).at[tuple(beside)].set(top_value)


def level_of(stream_key, extent, shards, least, top_value):
    loudness = 1.0
    for dim, shards_of in shards:
        heights = jax.random.uniform(jax.random.fold_in(jax.random.fold_in(stream_key, 6), dim), (shards_of,), jnp.float32, least / len(shards), top_value / len(shards))
        loudness = loudness * jnp.repeat(jnp.exp(heights), extent[dim] // shards_of).reshape((-1,) + (1,) * (len(extent) - 1 - dim))
    return loudness


def scatter_about(rng, shape, spread, most, pieces=(), held_as=jnp.bfloat16):
    gain = level_of(rng, shape, pieces, -0.22, 0.18) if pieces else 1.0
    values = jax.random.normal(rng, shape, jnp.float32) * spread * gain
    return jnp.minimum(jnp.maximum(values, -most), most).astype(held_as)


def setup_inputs(seed: int = 0) -> dict:
    key_list = jax.random.split(jax.random.key(seed), 10)
    return {
        "state": scatter_about(key_list[0], (AUXILIARIES, 2, M, M), 1.0, 6.0, ((0, 32),), jnp.float32),
        "h_static": scatter_about(key_list[1], (2, M, M), M ** -0.5, 0.375, (), jnp.float32),
        "drive_op": scatter_about(key_list[2], (2, M, M), M ** -0.5, 0.375, (), jnp.float32),
        "couple": scatter_about(key_list[3], (MODES, M, M), M ** -0.5, 0.375, (), jnp.float32),
        "bath_coef": jnp.clip(jax.random.uniform(key_list[4], (2, MODES), jnp.float32, -2.0, 2.0), -2.0, 2.0),
        "damping": jnp.clip(jnp.exp(jax.random.uniform(key_list[5], (MODES,), jnp.float32, math.log(0.3), math.log(3.0))), 0.3, 3.0),
        "occupation": place_ends(jax.random.randint(key_list[6], (AUXILIARIES, MODES), 1, 4), jax.random.fold_in(key_list[6], 1), 1, 3).astype(jnp.int32),
        "raise_nbr": draw_raise_nbr(jax.random.fold_in(key_list[9], 71), 0),
        "lower_nbr": draw_lower_nbr(jax.random.fold_in(key_list[9], 71), 0),
    }


HIGH = lax.Precision.HIGHEST
time_step = 0.05
drive_amp = 2.0
drive_freq = 20.0


def mul_left(matrix, batch):
    return jnp.einsum("ij,bjk->bik", matrix, batch, precision=HIGH)


def mul_right(batch, matrix):
    return jnp.einsum("bij,jk->bik", batch, matrix, precision=HIGH)


def hamil_comm(h_re, h_im, block):
    x_real = block[:, 0]
    x_imag = block[:, 1]
    comm_re = mul_left(h_re, x_real) - mul_left(h_im, x_imag) - mul_right(x_real, h_re) + mul_right(x_imag, h_im)
    comm_im = mul_left(h_re, x_imag) + mul_left(h_im, x_real) - mul_right(x_real, h_im) - mul_right(x_imag, h_re)
    return jnp.stack([comm_im, -comm_re], axis=1)


def derivative(block, raised, lowered, h_re, h_im, coupling, bath_coef, damping, level_counts):
    local_count = block.shape[0]
    rates = jnp.sum(level_counts * damping[None, :], axis=1)
    total = hamil_comm(h_re, h_im, block) - rates[:, None, None, None] * block
    for mode in range(coupling.shape[0]):
        stacked = jnp.concatenate([raised[:, mode], lowered[:, mode]], axis=0)
        flat = stacked.reshape((-1,) + stacked.shape[2:])
        q_times = mul_left(coupling[mode], flat).reshape(stacked.shape)
        times_q = mul_right(flat, coupling[mode]).reshape(stacked.shape)
        up_diff = q_times[:local_count] - times_q[:local_count]
        total = total + jnp.stack([up_diff[:, 1], -up_diff[:, 0]], axis=1)
        low_sum = q_times[local_count:] + times_q[local_count:]
        low_diff = q_times[local_count:] - times_q[local_count:]
        coef_re = bath_coef[0, mode]
        coef_im = bath_coef[1, mode]
        weight_n = level_counts[:, mode][:, None, None]
        part_re = weight_n * (coef_im * low_sum[:, 0] + coef_re * low_diff[:, 1])
        part_im = weight_n * (coef_im * low_sum[:, 1] - coef_re * low_diff[:, 0])
        total = total + jnp.stack([part_re, part_im], axis=1)
    return total


def reference(state, h_static, drive_op, couple, bath_coef, damping, occupation, raise_nbr, lower_nbr):
    h0_re = (h_static[0] + h_static[0].T) / 2
    h0_im = (h_static[1] - h_static[1].T) / 2
    dv_re = (drive_op[0] + drive_op[0].T) / 2
    dv_im = (drive_op[1] - drive_op[1].T) / 2
    coupling = (couple + jnp.swapaxes(couple, 1, 2)) / 2
    levels = occupation.astype(jnp.float32)

    def field(section_in, moment):
        drive_now = drive_amp * jnp.cos(jnp.float32(drive_freq * moment))
        h_re = h0_re + drive_now * dv_re
        h_im = h0_im + drive_now * dv_im

        def single(entries):
            block, up_list, down_list, level_row = entries
            up_ok = up_list >= 0
            down_ok = down_list >= 0
            raised = jnp.take(section_in, jnp.where(up_ok, up_list, 0).astype(jnp.int32), axis=0)
            raised = jnp.where(up_ok[:, None, None, None], raised, jnp.float32(0.0))
            lowered = jnp.take(section_in, jnp.where(down_ok, down_list, 0).astype(jnp.int32), axis=0)
            lowered = jnp.where(down_ok[:, None, None, None], lowered, jnp.float32(0.0))
            return derivative(block[None], raised[None], lowered[None], h_re, h_im, coupling, bath_coef, damping, level_row[None])[0]

        return lax.map(single, (section_in, raise_nbr, lower_nbr, levels))

    half = time_step / 2
    first = field(state, 0.0)
    second = field(state + half * first, half)
    third = field(state + half * second, half)
    fourth = field(state + time_step * third, time_step)
    return state + (time_step / 6) * (first + 2 * second + 2 * third + fourth)
```

```python
import math

import jax
import jax.numpy as jnp
from jax import lax
from jax.experimental import pallas as pl
from jax.experimental.pallas import tpu as pltpu
from jax.sharding import PartitionSpec as P

time_step = 0.05
drive_amp = 2.0
drive_freq = 20.0
META = 8
F32 = jnp.float32
BF16 = jnp.bfloat16
VMEM = pl.BlockSpec(memory_space=pltpu.VMEM)
SMEM = pl.BlockSpec(memory_space=pltpu.SMEM)


def chip_of(problem, block):
    group, odd = block >> 1, block & 1
    return group * 4 + ((odd ^ (group & 1)) << 1) + problem


def device_of(problem, block, pair):
    return chip_of(problem, block) * 2 + ((block & 1) ^ pair)


def role_of(device):
    core, problem, y, group = device & 1, (device >> 1) & 1, (device >> 2) & 1, device >> 3
    odd = y ^ (group & 1)
    return problem, 2 * group + odd, core ^ odd


def permutations(count):
    blocks = count // 4
    first, second, link = [], [], []
    for device in range(count):
        block, half, slot = device >> 2, (device >> 1) & 1, device & 1
        first.append((device, device_of(slot, block, half)))
        second.append((device, device_of(1 - slot, block, half)))
    for problem in range(2):
        for block in range(blocks - 1):
            here, there = device_of(problem, block, 1), device_of(problem, block + 1, 0)
            link += [(here, there), (there, here)]
    for block, pair in ((0, 0), (blocks - 1, 1)):
        here, there = device_of(0, block, pair), device_of(1, block, pair)
        link += [(here, there), (there, here)]
    core = [(device, device ^ 1) for device in range(count)]
    return first, second, sorted(link), core


def flipped(pairs):
    return sorted((b, a) for a, b in pairs)


def split(value):
    high = value.astype(BF16)
    return high, (value - high.astype(F32)).astype(BF16)


def store_stack(ref, index, w_re, w_im):
    size = w_re.shape[0]
    re_hi, re_lo = split(w_re)
    im_hi, im_lo = split(w_im)
    ref[index, 0:size] = re_hi
    ref[index, size : 2 * size] = im_hi
    ref[index, 2 * size : 3 * size] = re_lo
    ref[index, 3 * size : 4 * size] = im_lo


def dot_nn(a, b):
    return lax.dot_general(a, b, (((1,), (0,)), ((), ())), preferred_element_type=F32)


def dot_nt(a, b):
    return lax.dot_general(a, b, (((1,), (1,)), ((), ())), preferred_element_type=F32)


def products(stack, source):
    high, low = split(source)
    size = source.shape[0]
    both, top = stack[...], stack[0 : 2 * size]
    plain = dot_nn(both, high)
    plain = plain[: 2 * size] + plain[2 * size :] + dot_nn(top, low)
    turned = dot_nt(both, high)
    turned = turned[: 2 * size] + turned[2 * size :] + dot_nt(top, low)
    return plain[size:] - turned[:size], plain[:size] + turned[size:]


def role(axis):
    return role_of(lax.axis_index(axis))


def convert_kernel(state, occupation, raise_nbr, lower_nbr, first, second):
    slot = lax.axis_index("aux") & 1
    re, im = state[0, 0], state[0, 1]
    size = re.shape[0]
    total, diff = re + im, re - im
    herm = 0.5 * (total + diff.T)
    anti = 0.5 * (total.T - diff)
    first[0:size] = jnp.where(slot == 0, herm, anti)
    second[0:size] = jnp.where(slot == 0, anti, herm)
    lane = lax.broadcasted_iota(jnp.int32, (META, size), 1)
    modes = occupation.shape[1]
    row = jnp.zeros((META, size), F32)
    for mode in range(modes):
        for place, table in enumerate((occupation, raise_nbr, lower_nbr)):
            row = jnp.where(lane == place * modes + mode, table[0, mode].astype(F32), row)
    first[size : size + META] = row
    second[size : size + META] = row


def prepare_kernel(h_static, drive_op, couple, h_out, q_out):
    h_re = (h_static[0] + h_static[0].T) * 0.5
    h_im = (h_static[1] - h_static[1].T) * 0.5
    v_re = (drive_op[0] + drive_op[0].T) * 0.5
    v_im = (drive_op[1] - drive_op[1].T) * 0.5
    for index, moment in enumerate((0.0, time_step / 2, time_step)):
        drive = drive_amp * math.cos(drive_freq * moment)
        store_stack(h_out, index, h_re + drive * v_re, h_im + drive * v_im)
    for mode in range(couple.shape[0]):
        q_out[mode] = (couple[mode] + couple[mode].T) * 0.5


def weight_kernel(first, second, q_ref, bath_coef, damping, own_w, near_w, far_w, start, rate):
    problem, block, pair = role("aux")
    modes, size = q_ref.shape[0], q_ref.shape[1]
    is_first = problem == 0
    base = 4 * block + 2 * pair
    start[0] = jnp.where(is_first, first[0:size], second[0:size])
    start[1] = jnp.where(is_first, second[0:size], first[0:size])
    meta = []
    for slot in range(2):
        mine = jnp.where(is_first == (slot == 0), first[size : size + 1], second[size : size + 1])
        meta.append(mine)

    def entry(slot, place, mode):
        column = place * modes + mode
        return meta[slot][:, column : column + 1]

    for slot in range(2):
        total = jnp.zeros((1, 1), F32)
        for mode in range(modes):
            total = total + entry(slot, 0, mode) * damping[mode]
        rate[slot] = jnp.broadcast_to(total, rate.shape[1:])

    def weights(slot, source):
        source = jnp.where(source < 0, -9, source).astype(F32)
        w_re = jnp.zeros((size, size), F32)
        w_im = jnp.zeros((size, size), F32)
        for mode in range(modes):
            up = jnp.where(entry(slot, 1, mode) == source, 1.0, 0.0)
            down = jnp.where(entry(slot, 2, mode) == source, entry(slot, 0, mode), 0.0)
            q = q_ref[mode]
            w_re = w_re + (up + down * bath_coef[0, mode]) * q
            w_im = w_im + (down * bath_coef[1, mode]) * q
        return w_re, w_im

    def put(ref, index, slot, source):
        store_stack(ref, index, *weights(slot, source))

    put(own_w, 0, 0, base + 1)
    put(own_w, 1, 1, base)
    partner = base + jnp.where(pair == 0, 2, -2)
    other = base + jnp.where(pair == 0, -2, 2)
    for ref, where, lead in ((near_w, partner, pair), (far_w, other, 1 - pair)):
        for index, (here, there) in enumerate(((1 - lead, lead), (lead, lead), (1 - lead, 1 - lead))):
            w0 = weights(0, where + there)
            w1 = weights(1, where + there)
            pick = here == 0
            store_stack(ref, index, jnp.where(pick, w0[0], w1[0]), jnp.where(pick, w0[1], w1[1]))


def own_kernel(mine, h_ref, own_w, rate, out):
    x0, x1 = mine[0], mine[1]
    m00, p00 = products(h_ref.at[0], x0)
    m11, p11 = products(h_ref.at[0], x1)
    m01, p01 = products(own_w.at[0], x1)
    m10, p10 = products(own_w.at[1], x0)
    out[0, 0] = m00 + m01 - rate[0][0:1, 0:1] * x0
    out[0, 1] = p00 + p01
    out[1, 0] = m11 + m10 - rate[1][0:1, 0:1] * x1
    out[1, 1] = p11 + p10


def choose(refs, slot, problem, size):
    if len(refs) == 1:
        return refs[0][slot]
    return jnp.where(slot == problem, refs[0][0:size], refs[1][0:size])


def neighbour(refs, lead, problem, w_ref):
    size = w_ref.shape[2]
    near = choose(refs, lead, problem, size)
    far = choose(refs, 1 - lead, problem, size)
    m_a, p_a = products(w_ref.at[0], near)
    m_b, p_b = products(w_ref.at[1], near)
    m_c, p_c = products(w_ref.at[2], far)
    return m_a + m_c, p_a + p_c, m_b, p_b


def partner_kernel(count, *refs):
    sources, (near_w, early, out) = refs[:count], refs[count:]
    problem, _, pair = role("aux")
    lead = pair
    m_n, p_n, m_f, p_f = neighbour(sources, lead, problem, near_w)
    near, far = 1 - lead, lead
    out[near] = early[near, 0] + m_n + (early[near, 1] + p_n).T
    out[far] = early[far, 0] + m_f + (early[far, 1] + p_f).T


def link_kernel(count, step, weight, *refs):
    sources, (far_w, early, base, acc, out, acc_out) = refs[:count], refs[count:]
    problem, _, pair = role("aux")
    lead = 1 - pair
    m_n, p_n, m_f, p_f = neighbour(sources, lead, problem, far_w)
    for slot, m, p in ((1 - lead, m_n, p_n), (lead, m_f, p_f)):
        slope = early[slot] + m + p.T
        out[slot] = base[slot] + step * slope
        acc_out[slot] = acc[slot] + weight * slope


def last_kernel(weight, link, far_w, early, acc, first, second):
    problem, _, pair = role("aux")
    lead = 1 - pair
    m_n, p_n, m_f, p_f = neighbour((link,), lead, problem, far_w)
    near, far = 1 - lead, lead
    v_near = acc[near] + weight * (early[near] + m_n + p_n.T)
    v_far = acc[far] + weight * (early[far] + m_f + p_f.T)
    near_first = near == problem
    first[...] = jnp.where(near_first, v_near, v_far)
    second[...] = jnp.where(near_first, v_far, v_near)


def restore_kernel(first, second, out):
    slot = lax.axis_index("aux") & 1
    herm = jnp.where(slot == 0, first[...], second[...])
    anti = jnp.where(slot == 0, second[...], first[...])
    total = herm + anti.T
    diff = herm.T - anti
    out[0, 0] = 0.5 * (total + diff)
    out[0, 1] = 0.5 * (total - diff)


def call(kernel, out_shapes, args, smem=(), flops=0, name=None):
    shapes = [jax.ShapeDtypeStruct(shape, dtype) for shape, dtype in out_shapes]
    moved = sum(math.prod(a.shape) * a.dtype.itemsize for a in list(args) + shapes)
    single = len(shapes) == 1
    return pl.pallas_call(
        kernel,
        out_shape=shapes[0] if single else shapes,
        in_specs=[SMEM if index in smem else VMEM for index in range(len(args))],
        out_specs=VMEM if single else [VMEM] * len(shapes),
        cost_estimate=pl.CostEstimate(flops=flops, bytes_accessed=moved, transcendentals=0),
        compiler_params=pltpu.CompilerParams(vmem_limit_bytes=32 * 1024 * 1024),
        name=name,
    )(*args)


def on_device(state, h_static, drive_op, couple, bath_coef, damping, occupation, raise_nbr, lower_nbr):
    count = lax.axis_size("aux")
    size = state.shape[-1]
    modes = couple.shape[0]
    first_to, second_to, link_to, core_to = permutations(count)
    pair_shape = (2, size, size)
    unit = 2 * size**3

    def send(value, pairs):
        return lax.ppermute(value, "aux", pairs)

    tall = ((size + META, size), F32)
    first, second = call(
        convert_kernel, [tall, tall], [state, occupation, raise_nbr, lower_nbr], smem=(1, 2, 3), name="convert"
    )
    first, second = send(first, first_to), send(second, second_to)
    stacks, q_all = call(
        prepare_kernel,
        [((3, 4 * size, size), BF16), ((modes, size, size), F32)],
        [h_static, drive_op, couple],
        name="prepare",
    )
    h_now = [stacks[index : index + 1] for index in range(3)]

    link = (send(first, link_to), send(second, link_to))
    partner = (send(first, core_to), send(second, core_to))
    own_w, near_w, far_w, base, rate = call(
        weight_kernel,
        [((2, 4 * size, size), BF16), ((3, 4 * size, size), BF16), ((3, 4 * size, size), BF16), (pair_shape, F32),
         ((2, 8, 128), F32)],
        [first, second, q_all, bath_coef, damping],
        smem=(3, 4),
        flops=20 * unit,
        name="weights",
    )
    current, acc = base, base
    steps = (time_step / 2, time_step / 2, time_step)
    weights = (time_step / 6, time_step / 3, time_step / 3)
    for stage in range(4):
        if stage:
            link = (send(current, link_to),)
            partner = (send(current, core_to),)
        early = call(
            own_kernel,
            [((2, 2, size, size), F32)],
            [current, h_now[(0, 1, 1, 2)[stage]], own_w, rate],
            flops=48 * unit,
            name=f"own{stage}",
        )
        early = call(
            lambda *refs, n=len(partner): partner_kernel(n, *refs),
            [(pair_shape, F32)],
            [*partner, near_w, early],
            flops=36 * unit,
            name=f"partner{stage}",
        )
        if stage < 3:
            current, acc = call(
                lambda *refs, n=len(link), s=steps[stage], w=weights[stage]: link_kernel(n, s, w, *refs),
                [(pair_shape, F32), (pair_shape, F32)],
                [*link, far_w, early, base, acc],
                flops=36 * unit,
                name=f"link{stage}",
            )
    flat = ((size, size), F32)
    first, second = call(
        lambda *refs: last_kernel(time_step / 6, *refs),
        [flat, flat],
        [*link, far_w, early, acc],
        flops=36 * unit,
        name="last",
    )
    first, second = send(first, flipped(first_to)), send(second, flipped(second_to))
    return call(restore_kernel, [((1, 2, size, size), F32)], [first, second], name="restore")


def solution(mesh):
    return jax.shard_map(
        on_device,
        mesh=mesh,
        in_specs=(
            P("aux", None, None, None),
            P(),
            P(),
            P(),
            P(),
            P(),
            P("aux", None),
            P("aux", None),
            P("aux", None),
        ),
        out_specs=P("aux", None, None, None),
        check_vma=False,
    )
```

```python
import math

import jax
import jax.numpy as jnp
from jax import lax
from jax.experimental import pallas as pl
from jax.experimental.pallas import tpu as pltpu
from jax.sharding import PartitionSpec as P

time_step = 0.05
drive_amp = 2.0
drive_freq = 20.0
META = 8
F32 = jnp.float32
BF16 = jnp.bfloat16
VMEM = pl.BlockSpec(memory_space=pltpu.VMEM)
SMEM = pl.BlockSpec(memory_space=pltpu.SMEM)


def chip_of(problem, block):
    group, odd = block >> 1, block & 1
    return group * 4 + problem * 2 + (odd ^ (group & 1))


def device_of(problem, block, pair):
    return chip_of(problem, block) * 2 + ((block & 1) ^ pair)


def role_of(device):
    core, x, problem, group = device & 1, (device >> 1) & 1, (device >> 2) & 1, device >> 3
    odd = x ^ (group & 1)
    return problem, 2 * group + odd, core ^ odd


def permutations(count):
    blocks = count // 4
    first, second, link = [], [], []
    for device in range(count):
        block, half, slot = device >> 2, (device >> 1) & 1, device & 1
        first.append((device, device_of(slot, block, half)))
        second.append((device, device_of(1 - slot, block, half)))
    for problem in range(2):
        for block in range(blocks - 1):
            here, there = device_of(problem, block, 1), device_of(problem, block + 1, 0)
            link += [(here, there), (there, here)]
    for block, pair in ((0, 0), (blocks - 1, 1)):
        here, there = device_of(0, block, pair), device_of(1, block, pair)
        link += [(here, there), (there, here)]
    core = [(device, device ^ 1) for device in range(count)]
    return first, second, sorted(link), core


def flipped(pairs):
    return sorted((b, a) for a, b in pairs)


def split(value):
    high = value.astype(BF16)
    return high, (value - high.astype(F32)).astype(BF16)


def store_stack(ref, index, w_re, w_im):
    size = w_re.shape[0]
    for place, value in enumerate((w_re, w_im, w_re + w_im)):
        high, low = split(value)
        ref[index, 2 * place * size : (2 * place + 1) * size] = high
        ref[index, (2 * place + 1) * size : (2 * place + 2) * size] = low


def dot_nn(a, b):
    return lax.dot_general(a, b, (((1,), (0,)), ((), ())), preferred_element_type=F32)


def dot_nt(a, b):
    return lax.dot_general(a, b, (((1,), (1,)), ((), ())), preferred_element_type=F32)


def three(stack, place, source, dot):
    high, low = source
    size = high.shape[0]
    both = stack[2 * place * size : (2 * place + 2) * size]
    wide = dot(both, high)
    return wide[:size] + wide[size:] + dot(both[:size], low)


def forms(source, full):
    if not full:
        return (split(source),)
    turned = source.T
    return split(source), split(source + turned), split(source - turned)


def products(stack, source):
    if len(source) == 1:
        return -three(stack, 0, source[0], dot_nt), three(stack, 0, source[0], dot_nn)
    shared = three(stack, 2, source[0], dot_nn)
    return shared - three(stack, 0, source[1], dot_nn), shared - three(stack, 1, source[2], dot_nn)


def role(axis):
    return role_of(lax.axis_index(axis))


def by_type(lower, body):
    @pl.when(lower)
    def _():
        body(True)

    @pl.when(jnp.logical_not(lower))
    def _():
        body(False)


def convert_kernel(state_hbm, occ_hbm, up_hbm, low_hbm, first, second, state, occ, up, low, sems):
    copies = [
        pltpu.make_async_copy(src, dst, sems.at[index])
        for index, (src, dst) in enumerate(((state_hbm, state), (occ_hbm, occ), (up_hbm, up), (low_hbm, low)))
    ]
    for copy in copies:
        copy.start()
    for copy in copies:
        copy.wait()
    slot = lax.axis_index("aux") & 1
    re, im = state[0, 0], state[0, 1]
    size = re.shape[0]
    total, diff = re + im, re - im
    herm = 0.5 * (total + diff.T)
    anti = 0.5 * (total.T - diff)
    first[0:size] = jnp.where(slot == 0, herm, anti)
    second[0:size] = jnp.where(slot == 0, anti, herm)
    lane = lax.broadcasted_iota(jnp.int32, (META, size), 1)
    modes = occ.shape[1]
    row = jnp.zeros((META, size), F32)
    for mode in range(modes):
        for place, table in enumerate((occ, up, low)):
            row = jnp.where(lane == place * modes + mode, table[0, mode].astype(F32), row)
    first[size : size + META] = row
    second[size : size + META] = row


def prepare_kernel(h_static, drive_op, couple, h_out, q_out):
    h_re = (h_static[0] + h_static[0].T) * 0.5
    h_im = (h_static[1] - h_static[1].T) * 0.5
    v_re = (drive_op[0] + drive_op[0].T) * 0.5
    v_im = (drive_op[1] - drive_op[1].T) * 0.5
    for index, moment in enumerate((0.0, time_step / 2, time_step)):
        drive = drive_amp * math.cos(drive_freq * moment)
        store_stack(h_out, index, h_re + drive * v_re, h_im + drive * v_im)
    for mode in range(couple.shape[0]):
        q_out[mode] = (couple[mode] + couple[mode].T) * 0.5


def weight_kernel(first, second, q_ref, bath_coef, damping, own_w, partner_w, link_w, start, rate):
    problem, block, pair = role("aux")
    modes, size = q_ref.shape[0], q_ref.shape[1]
    near_first = pair == problem
    start[0] = jnp.where(near_first, first[0:size], second[0:size])
    start[1] = jnp.where(near_first, second[0:size], first[0:size])
    rows = (first[size : size + 1], second[size : size + 1])
    meta = (jnp.where(near_first, rows[0], rows[1]), jnp.where(near_first, rows[1], rows[0]))

    def entry(part, place, mode):
        column = place * modes + mode
        return meta[part][:, column : column + 1]

    for part in range(2):
        total = jnp.zeros((1, 1), F32)
        for mode in range(modes):
            total = total + entry(part, 0, mode) * damping[mode]
        rate[part] = jnp.broadcast_to(total, rate.shape[1:])

    def put(ref, index, part, source):
        source = jnp.where(source < 0, -9, source).astype(F32)
        w_re = jnp.zeros((size, size), F32)
        w_im = jnp.zeros((size, size), F32)
        for mode in range(modes):
            up = jnp.where(entry(part, 1, mode) == source, 1.0, 0.0)
            down = jnp.where(entry(part, 2, mode) == source, entry(part, 0, mode), 0.0)
            q = q_ref[mode]
            w_re = w_re + (up + down * bath_coef[0, mode]) * q
            w_im = w_im + (down * bath_coef[1, mode]) * q
        store_stack(ref, index, w_re, w_im)

    near = 4 * block + 3 * pair
    inward = 1 - 2 * pair
    far = near + inward
    put(own_w, 0, 0, far)
    put(own_w, 1, 1, near)
    put(link_w, 0, 0, near - inward)
    put(link_w, 1, 1, near - inward)
    put(link_w, 2, 0, near - 2 * inward)
    put(partner_w, 0, 1, far + inward)
    put(partner_w, 1, 0, far + inward)
    put(partner_w, 2, 1, far + 2 * inward)


def own_kernel(mine, h_ref, own_w, rate, out):
    _, _, pair = role("aux")
    near, far = mine[0], mine[1]
    near_forms, far_forms = forms(near, True), forms(far, True)
    m_n, p_n = products(h_ref.at[0], near_forms)
    m_f, p_f = products(h_ref.at[0], far_forms)
    m_n = m_n - rate[0][0:1, 0:1] * near
    m_f = m_f - rate[1][0:1, 0:1] * far

    def body(lower):
        m_nf, p_nf = products(own_w.at[0], far_forms if lower else far_forms[:1])
        m_fn, p_fn = products(own_w.at[1], near_forms[:1] if lower else near_forms)
        out[0] = m_n + m_nf + (p_n + p_nf).T
        out[1] = m_f + m_fn + (p_f + p_fn).T

    by_type(pair == 1, body)


def pick(refs, problem, pair, size):
    if len(refs) == 1:
        return refs[0][0], refs[0][1]
    near_first = pair == problem
    one, two = refs[0][0:size], refs[1][0:size]
    return jnp.where(near_first, one, two), jnp.where(near_first, two, one)


def outside(lead, other, w_ref, lower):
    lead, other = forms(lead, lower), forms(other, lower)
    m_a, p_a = products(w_ref.at[0], lead)
    m_b, p_b = products(w_ref.at[1], lead)
    m_c, p_c = products(w_ref.at[2], other)
    return m_a + m_c + (p_a + p_c).T, m_b + p_b.T


def partner_kernel(count, *refs):
    sources, (partner_w, early, out) = refs[:count], refs[count:]
    problem, _, pair = role("aux")
    near, far = pick(sources, problem, 1 - pair, partner_w.shape[2])

    def body(lower):
        to_far, to_near = outside_partner(near, far, partner_w, lower)
        out[0] = early[0] + to_near
        out[1] = early[1] + to_far

    by_type(pair == 1, body)


def outside_partner(near, far, w_ref, lower):
    lead, other = forms(far, lower), forms(near, lower)
    m_a, p_a = products(w_ref.at[0], lead)
    m_b, p_b = products(w_ref.at[1], lead)
    m_c, p_c = products(w_ref.at[2], other)
    return m_a + m_c + (p_a + p_c).T, m_b + p_b.T


def link_kernel(count, step, weight, *refs):
    sources, (link_w, early, base, acc, out, acc_out) = refs[:count], refs[count:]
    problem, _, pair = role("aux")
    near, far = pick(sources, problem, 1 - pair, link_w.shape[2])

    def body(lower):
        terms = outside(near, far, link_w, lower)
        for part in range(2):
            slope = early[part] + terms[part]
            out[part] = base[part] + step * slope
            acc_out[part] = acc[part] + weight * slope

    by_type(pair == 0, body)


def last_kernel(weight, link, link_w, early, acc, first, second):
    problem, _, pair = role("aux")
    near_first = pair == problem

    def body(lower):
        terms = outside(link[0], link[1], link_w, lower)
        near = acc[0] + weight * (early[0] + terms[0])
        far = acc[1] + weight * (early[1] + terms[1])
        first[...] = jnp.where(near_first, near, far)
        second[...] = jnp.where(near_first, far, near)

    by_type(pair == 0, body)


def restore_kernel(first, second, out):
    slot = lax.axis_index("aux") & 1
    herm = jnp.where(slot == 0, first[...], second[...])
    anti = jnp.where(slot == 0, second[...], first[...])
    total = herm + anti.T
    diff = herm.T - anti
    out[0, 0] = 0.5 * (total + diff)
    out[0, 1] = 0.5 * (total - diff)


def call(kernel, out_shapes, args, smem=(), flops=0, name=None, space=None, scratch=()):
    shapes = [jax.ShapeDtypeStruct(shape, dtype) for shape, dtype in out_shapes]
    moved = sum(math.prod(a.shape) * a.dtype.itemsize for a in list(args) + shapes)
    single = len(shapes) == 1
    return pl.pallas_call(
        kernel,
        out_shape=shapes[0] if single else shapes,
        in_specs=[space or (SMEM if index in smem else VMEM) for index in range(len(args))],
        out_specs=VMEM if single else [VMEM] * len(shapes),
        scratch_shapes=scratch,
        cost_estimate=pl.CostEstimate(flops=flops, bytes_accessed=moved, transcendentals=0),
        compiler_params=pltpu.CompilerParams(vmem_limit_bytes=32 * 1024 * 1024),
        name=name,
    )(*args)


def on_device(state, h_static, drive_op, couple, bath_coef, damping, occupation, raise_nbr, lower_nbr):
    count = lax.axis_size("aux")
    size = state.shape[-1]
    modes = couple.shape[0]
    first_to, second_to, link_to, core_to = permutations(count)
    pair_shape = (2, size, size)
    unit = 2 * size**3

    def send(value, pairs):
        return lax.ppermute(value, "aux", pairs)

    tall = ((size + META, size), F32)
    tables = [occupation, raise_nbr, lower_nbr]
    first, second = call(
        convert_kernel,
        [tall, tall],
        [state] + tables,
        name="convert",
        space=pl.BlockSpec(memory_space=pltpu.HBM),
        scratch=[pltpu.VMEM(state.shape, F32)]
        + [pltpu.SMEM(table.shape, jnp.int32) for table in tables]
        + [pltpu.SemaphoreType.DMA((4,))],
    )
    first, second = send(first, first_to), send(second, second_to)
    stacks, q_all = call(
        prepare_kernel,
        [((3, 6 * size, size), BF16), ((modes, size, size), F32)],
        [h_static, drive_op, couple],
        name="prepare",
    )
    h_now = [stacks[index : index + 1] for index in range(3)]

    link = (send(first, link_to), send(second, link_to))
    partner = (send(first, core_to), send(second, core_to))
    own_w, partner_w, link_w, base, rate = call(
        weight_kernel,
        [((2, 6 * size, size), BF16), ((3, 6 * size, size), BF16), ((3, 6 * size, size), BF16), (pair_shape, F32),
         ((2, 8, 128), F32)],
        [first, second, q_all, bath_coef, damping],
        smem=(3, 4),
        flops=20 * unit,
        name="weights",
    )
    current, acc = base, base
    steps = (time_step / 2, time_step / 2, time_step)
    weights = (time_step / 6, time_step / 3, time_step / 3)
    for stage in range(4):
        if stage:
            link = (send(current, link_to),)
            partner = (send(current, core_to),)
        early = call(
            own_kernel,
            [(pair_shape, F32)],
            [current, h_now[(0, 1, 1, 2)[stage]], own_w, rate],
            flops=33 * unit,
            name=f"own{stage}",
        )
        early = call(
            lambda *refs, n=len(partner): partner_kernel(n, *refs),
            [(pair_shape, F32)],
            [*partner, partner_w, early],
            flops=27 * unit,
            name=f"partner{stage}",
        )
        if stage < 3:
            current, acc = call(
                lambda *refs, n=len(link), s=steps[stage], w=weights[stage]: link_kernel(n, s, w, *refs),
                [(pair_shape, F32), (pair_shape, F32)],
                [*link, link_w, early, base, acc],
                flops=27 * unit,
                name=f"link{stage}",
            )
    flat = ((size, size), F32)
    first, second = call(
        lambda *refs: last_kernel(time_step / 6, *refs),
        [flat, flat],
        [*link, link_w, early, acc],
        flops=27 * unit,
        name="last",
    )
    first, second = send(first, flipped(first_to)), send(second, flipped(second_to))
    return call(restore_kernel, [((1, 2, size, size), F32)], [first, second], name="restore")


def solution(mesh):
    return jax.shard_map(
        on_device,
        mesh=mesh,
        in_specs=(
            P("aux", None, None, None),
            P(),
            P(),
            P(),
            P(),
            P(),
            P("aux", None),
            P("aux", None),
            P("aux", None),
        ),
        out_specs=P("aux", None, None, None),
        check_vma=False,
    )
```

```python
import math

import jax
import jax.numpy as jnp
from jax import lax
from jax.experimental import pallas as pl
from jax.experimental.pallas import tpu as pltpu
from jax.sharding import PartitionSpec as P

time_step = 0.05
drive_amp = 2.0
drive_freq = 20.0
META = 8
F32 = jnp.float32
BF16 = jnp.bfloat16
VMEM = pl.BlockSpec(memory_space=pltpu.VMEM)
SMEM = pl.BlockSpec(memory_space=pltpu.SMEM)


def chip_of(problem, block):
    group, odd = block >> 1, block & 1
    return group * 4 + problem * 2 + (odd ^ (group & 1))


def device_of(problem, block, pair):
    return chip_of(problem, block) * 2 + ((block & 1) ^ pair)


def role_of(device):
    core, x, problem, group = device & 1, (device >> 1) & 1, (device >> 2) & 1, device >> 3
    odd = x ^ (group & 1)
    return problem, 2 * group + odd, core ^ odd


def permutations(count):
    blocks = count // 4
    first, second, link = [], [], []
    for device in range(count):
        block, half, slot = device >> 2, (device >> 1) & 1, device & 1
        first.append((device, device_of(slot, block, half)))
        second.append((device, device_of(1 - slot, block, half)))
    for problem in range(2):
        for block in range(blocks - 1):
            here, there = device_of(problem, block, 1), device_of(problem, block + 1, 0)
            link += [(here, there), (there, here)]
    for block, pair in ((0, 0), (blocks - 1, 1)):
        here, there = device_of(0, block, pair), device_of(1, block, pair)
        link += [(here, there), (there, here)]
    core = [(device, device ^ 1) for device in range(count)]
    return first, second, sorted(link), core


def flipped(pairs):
    return sorted((b, a) for a, b in pairs)


def split(value):
    high = value.astype(BF16)
    return high, (value - high.astype(F32)).astype(BF16)


def store_stack(ref, index, w_re, w_im=None):
    size = w_re.shape[0]
    for place, value in enumerate((w_re,) if w_im is None else (w_re, w_im, w_re + w_im)):
        high, low = split(value)
        ref[index, 2 * place * size : (2 * place + 1) * size] = high
        ref[index, (2 * place + 1) * size : (2 * place + 2) * size] = low


def dot_nn(a, b):
    return lax.dot_general(a, b, (((1,), (0,)), ((), ())), preferred_element_type=F32)


def dot_nt(a, b):
    return lax.dot_general(a, b, (((1,), (1,)), ((), ())), preferred_element_type=F32)


def three(stack, place, source, dot):
    high, low = source
    size = high.shape[0]
    both = stack[2 * place * size : (2 * place + 2) * size]
    wide = dot(both, high)
    return wide[:size] + wide[size:] + dot(both[:size], low)


def forms(source, full):
    if not full:
        return (split(source),)
    turned = source.T
    return split(source), split(source + turned), split(source - turned)


def products(stack, source):
    if len(source) == 1:
        return -three(stack, 0, source[0], dot_nt), three(stack, 0, source[0], dot_nn)
    shared = three(stack, 2, source[0], dot_nn)
    return shared - three(stack, 0, source[1], dot_nn), shared - three(stack, 1, source[2], dot_nn)


def role(axis):
    return role_of(lax.axis_index(axis))


def by_type(lower, body):
    @pl.when(lower)
    def _():
        body(True)

    @pl.when(jnp.logical_not(lower))
    def _():
        body(False)


def convert_kernel(state_hbm, occ_hbm, up_hbm, low_hbm, first, second, state, occ, up, low, sems):
    copies = [
        pltpu.make_async_copy(src, dst, sems.at[index])
        for index, (src, dst) in enumerate(((state_hbm, state), (occ_hbm, occ), (up_hbm, up), (low_hbm, low)))
    ]
    for copy in copies:
        copy.start()
    for copy in copies:
        copy.wait()
    slot = lax.axis_index("aux") & 1
    re, im = state[0, 0], state[0, 1]
    size = re.shape[0]
    total, diff = re + im, re - im
    herm = 0.5 * (total + diff.T)
    anti = 0.5 * (total.T - diff)
    first[0:size] = jnp.where(slot == 0, herm, anti)
    second[0:size] = jnp.where(slot == 0, anti, herm)
    lane = lax.broadcasted_iota(jnp.int32, (META, size), 1)
    modes = occ.shape[1]
    row = jnp.zeros((META, size), F32)
    for mode in range(modes):
        for place, table in enumerate((occ, up, low)):
            row = jnp.where(lane == place * modes + mode, table[0, mode].astype(F32), row)
    first[size : size + META] = row
    second[size : size + META] = row


def prepare_kernel(h_static, drive_op, couple, h_out, q_out):
    h_re = (h_static[0] + h_static[0].T) * 0.5
    h_im = (h_static[1] - h_static[1].T) * 0.5
    v_re = (drive_op[0] + drive_op[0].T) * 0.5
    v_im = (drive_op[1] - drive_op[1].T) * 0.5
    for index, moment in enumerate((0.0, time_step / 2, time_step)):
        drive = drive_amp * math.cos(drive_freq * moment)
        store_stack(h_out, index, h_re + drive * v_re, h_im + drive * v_im)
    for mode in range(couple.shape[0]):
        q_out[mode] = (couple[mode] + couple[mode].T) * 0.5


def weight_kernel(first, second, q_ref, bath_coef, damping, own_w, partner_w, link_w, start, rate):
    problem, block, pair = role("aux")
    modes, size = q_ref.shape[0], q_ref.shape[1]
    near_first = pair == problem
    start[0] = jnp.where(near_first, first[0:size], second[0:size])
    start[1] = jnp.where(near_first, second[0:size], first[0:size])
    rows = (first[size : size + 1], second[size : size + 1])
    meta = (jnp.where(near_first, rows[0], rows[1]), jnp.where(near_first, rows[1], rows[0]))

    def entry(part, place, mode):
        column = place * modes + mode
        return meta[part][:, column : column + 1]

    for part in range(2):
        total = jnp.zeros((1, 1), F32)
        for mode in range(modes):
            total = total + entry(part, 0, mode) * damping[mode]
        rate[part] = jnp.broadcast_to(total, rate.shape[1:])

    def put(lower, ref, index, part, source):
        source = jnp.where(source < 0, -9, source).astype(F32)
        w_re = w_im = None
        for mode in range(modes):
            hit = entry(part, 2 if lower else 1, mode) == source
            q = q_ref[mode]
            if lower:
                down = jnp.where(hit, entry(part, 0, mode), 0.0)
                im = (down * bath_coef[1, mode]) * q
                w_im = im if w_im is None else w_im + im
                re = (down * bath_coef[0, mode]) * q
            else:
                re = jnp.where(hit, 1.0, 0.0) * q
            w_re = re if w_re is None else w_re + re
        store_stack(ref, index, w_re, w_im)

    near = 4 * block + 3 * pair
    inward = 1 - 2 * pair
    far = near + inward

    def body(lower):
        put(not lower, own_w, 0, 0, far)
        put(lower, own_w, 1, 1, near)
        put(lower, link_w, 0, 0, near - inward)
        put(lower, link_w, 1, 1, near - inward)
        put(lower, link_w, 2, 0, near - 2 * inward)
        put(not lower, partner_w, 0, 1, far + inward)
        put(not lower, partner_w, 1, 0, far + inward)
        put(not lower, partner_w, 2, 1, far + 2 * inward)

    by_type(pair == 0, body)


def own_kernel(mine, h_ref, own_w, rate, out):
    _, _, pair = role("aux")
    near, far = mine[0], mine[1]
    near_forms, far_forms = forms(near, True), forms(far, True)
    m_n, p_n = products(h_ref.at[0], near_forms)
    m_f, p_f = products(h_ref.at[0], far_forms)
    m_n = m_n - rate[0][0:1, 0:1] * near
    m_f = m_f - rate[1][0:1, 0:1] * far

    def body(lower):
        m_nf, p_nf = products(own_w.at[0], far_forms if lower else far_forms[:1])
        m_fn, p_fn = products(own_w.at[1], near_forms[:1] if lower else near_forms)
        out[0] = m_n + m_nf + (p_n + p_nf).T
        out[1] = m_f + m_fn + (p_f + p_fn).T

    by_type(pair == 1, body)


def pick(refs, problem, pair, size):
    if len(refs) == 1:
        return refs[0][0], refs[0][1]
    near_first = pair == problem
    one, two = refs[0][0:size], refs[1][0:size]
    return jnp.where(near_first, one, two), jnp.where(near_first, two, one)


def outside(lead, other, w_ref, lower):
    lead, other = forms(lead, lower), forms(other, lower)
    m_a, p_a = products(w_ref.at[0], lead)
    m_b, p_b = products(w_ref.at[1], lead)
    m_c, p_c = products(w_ref.at[2], other)
    return m_a + m_c + (p_a + p_c).T, m_b + p_b.T


def partner_kernel(count, *refs):
    sources, (partner_w, early, out) = refs[:count], refs[count:]
    problem, _, pair = role("aux")
    near, far = pick(sources, problem, 1 - pair, partner_w.shape[2])

    def body(lower):
        to_far, to_near = outside_partner(near, far, partner_w, lower)
        out[0] = early[0] + to_near
        out[1] = early[1] + to_far

    by_type(pair == 1, body)


def outside_partner(near, far, w_ref, lower):
    lead, other = forms(far, lower), forms(near, lower)
    m_a, p_a = products(w_ref.at[0], lead)
    m_b, p_b = products(w_ref.at[1], lead)
    m_c, p_c = products(w_ref.at[2], other)
    return m_a + m_c + (p_a + p_c).T, m_b + p_b.T


def link_kernel(count, step, weight, *refs):
    sources, (link_w, early, base, acc, out, acc_out) = refs[:count], refs[count:]
    problem, _, pair = role("aux")
    near, far = pick(sources, problem, 1 - pair, link_w.shape[2])

    def body(lower):
        terms = outside(near, far, link_w, lower)
        for part in range(2):
            slope = early[part] + terms[part]
            out[part] = base[part] + step * slope
            acc_out[part] = acc[part] + weight * slope

    by_type(pair == 0, body)


def last_kernel(weight, link, link_w, early, acc, first, second):
    problem, _, pair = role("aux")
    near_first = pair == problem

    def body(lower):
        terms = outside(link[0], link[1], link_w, lower)
        near = acc[0] + weight * (early[0] + terms[0])
        far = acc[1] + weight * (early[1] + terms[1])
        first[...] = jnp.where(near_first, near, far)
        second[...] = jnp.where(near_first, far, near)

    by_type(pair == 0, body)


def restore_kernel(first, second, out):
    slot = lax.axis_index("aux") & 1
    herm = jnp.where(slot == 0, first[...], second[...])
    anti = jnp.where(slot == 0, second[...], first[...])
    total = herm + anti.T
    diff = herm.T - anti
    out[0, 0] = 0.5 * (total + diff)
    out[0, 1] = 0.5 * (total - diff)


def call(kernel, out_shapes, args, smem=(), flops=0, name=None, space=None, scratch=(), grant=32):
    shapes = [jax.ShapeDtypeStruct(shape, dtype) for shape, dtype in out_shapes]
    moved = sum(math.prod(a.shape) * a.dtype.itemsize for a in list(args) + shapes)
    single = len(shapes) == 1
    return pl.pallas_call(
        kernel,
        out_shape=shapes[0] if single else shapes,
        in_specs=[space or (SMEM if index in smem else VMEM) for index in range(len(args))],
        out_specs=VMEM if single else [VMEM] * len(shapes),
        scratch_shapes=scratch,
        cost_estimate=pl.CostEstimate(flops=flops, bytes_accessed=moved, transcendentals=0),
        compiler_params=pltpu.CompilerParams(vmem_limit_bytes=grant * 1024 * 1024),
        name=name,
    )(*args)


def on_device(state, h_static, drive_op, couple, bath_coef, damping, occupation, raise_nbr, lower_nbr):
    count = lax.axis_size("aux")
    size = state.shape[-1]
    modes = couple.shape[0]
    first_to, second_to, link_to, core_to = permutations(count)
    pair_shape = (2, size, size)
    unit = 2 * size**3

    def send(value, pairs):
        return lax.ppermute(value, "aux", pairs)

    tall = ((size + META, size), F32)
    tables = [occupation, raise_nbr, lower_nbr]
    first, second = call(
        convert_kernel,
        [tall, tall],
        [state] + tables,
        name="convert",
        space=pl.BlockSpec(memory_space=pltpu.HBM),
        grant=60,
        scratch=[pltpu.VMEM(state.shape, F32)]
        + [pltpu.SMEM(table.shape, jnp.int32) for table in tables]
        + [pltpu.SemaphoreType.DMA((4,))],
    )
    first, second = send(first, first_to), send(second, second_to)
    stacks, q_all = call(
        prepare_kernel,
        [((3, 6 * size, size), BF16), ((modes, size, size), F32)],
        [h_static, drive_op, couple],
        name="prepare",
    )
    h_now = [stacks[index : index + 1] for index in range(3)]

    link = (send(first, link_to), send(second, link_to))
    partner = (send(first, core_to), send(second, core_to))
    own_w, partner_w, link_w, base, rate = call(
        weight_kernel,
        [((2, 6 * size, size), BF16), ((3, 6 * size, size), BF16), ((3, 6 * size, size), BF16), (pair_shape, F32),
         ((2, 8, 128), F32)],
        [first, second, q_all, bath_coef, damping],
        smem=(3, 4),
        flops=20 * unit,
        name="weights",
    )
    current, acc = base, base
    steps = (time_step / 2, time_step / 2, time_step)
    weights = (time_step / 6, time_step / 3, time_step / 3)
    for stage in range(4):
        if stage:
            link = (send(current, link_to),)
            partner = (send(current, core_to),)
        early = call(
            own_kernel,
            [(pair_shape, F32)],
            [current, h_now[(0, 1, 1, 2)[stage]], own_w, rate],
            flops=33 * unit,
            name=f"own{stage}",
        )
        early = call(
            lambda *refs, n=len(partner): partner_kernel(n, *refs),
            [(pair_shape, F32)],
            [*partner, partner_w, early],
            flops=27 * unit,
            name=f"partner{stage}",
        )
        if stage < 3:
            current, acc = call(
                lambda *refs, n=len(link), s=steps[stage], w=weights[stage]: link_kernel(n, s, w, *refs),
                [(pair_shape, F32), (pair_shape, F32)],
                [*link, link_w, early, base, acc],
                flops=27 * unit,
                name=f"link{stage}",
            )
    flat = ((size, size), F32)
    first, second = call(
        lambda *refs: last_kernel(time_step / 6, *refs),
        [flat, flat],
        [*link, link_w, early, acc],
        flops=27 * unit,
        name="last",
    )
    first, second = send(first, flipped(first_to)), send(second, flipped(second_to))
    return call(restore_kernel, [((1, 2, size, size), F32)], [first, second], name="restore")


def solution(mesh):
    return jax.shard_map(
        on_device,
        mesh=mesh,
        in_specs=(
            P("aux", None, None, None),
            P(),
            P(),
            P(),
            P(),
            P(),
            P("aux", None),
            P("aux", None),
            P("aux", None),
        ),
        out_specs=P("aux", None, None, None),
        check_vma=False,
    )
```

```python
import math
from functools import partial

import jax
import jax.numpy as jnp
from jax import lax
from jax.experimental import pallas as pl
from jax.experimental.pallas import tpu as pltpu
from jax.sharding import PartitionSpec as P


time_step = 0.05
drive_amp = 2.0
drive_freq = 20.0
META = 8
F32 = jnp.float32
BF16 = jnp.bfloat16
VMEM = pl.BlockSpec(memory_space=pltpu.VMEM)
SMEM = pl.BlockSpec(memory_space=pltpu.SMEM)


def chip_of(problem, block):
    group, odd = block >> 1, block & 1
    return group * 4 + problem * 2 + (odd ^ (group & 1))


def device_of(problem, block, pair):
    return chip_of(problem, block) * 2 + ((block & 1) ^ pair)


def role_of(device):
    core, x, problem, group = device & 1, (device >> 1) & 1, (device >> 2) & 1, device >> 3
    odd = x ^ (group & 1)
    return problem, 2 * group + odd, core ^ odd


def permutations(count):
    blocks = count // 4
    first, second, link = [], [], []
    for device in range(count):
        block, half, slot = device >> 2, (device >> 1) & 1, device & 1
        first.append((device, device_of(slot, block, half)))
        second.append((device, device_of(1 - slot, block, half)))
    for problem in range(2):
        for block in range(blocks - 1):
            here, there = device_of(problem, block, 1), device_of(problem, block + 1, 0)
            link += [(here, there), (there, here)]
    for block, pair in ((0, 0), (blocks - 1, 1)):
        here, there = device_of(0, block, pair), device_of(1, block, pair)
        link += [(here, there), (there, here)]
    core = [(device, device ^ 1) for device in range(count)]
    return full(first), full(second), sorted(link), core


def full(pairs):
    fixed = [a for a, b in pairs if a == b]
    swaps = dict(zip(fixed[::2], fixed[1::2]))
    swaps.update({b: a for a, b in swaps.items()})
    return [(a, swaps.get(a, b)) for a, b in pairs]


def kept(device):
    block, half, slot = device >> 2, (device >> 1) & 1, device & 1
    return device_of(slot, block, half) == device, device_of(1 - slot, block, half) == device


def flipped(pairs):
    return sorted((b, a) for a, b in pairs)


def split(value):
    high = value.astype(BF16)
    return high, (value - high.astype(F32)).astype(BF16)


def store_stack(ref, index, w_re, w_im=None):
    size = w_re.shape[0]
    for place, value in enumerate((w_re,) if w_im is None else (w_re, w_im, w_re + w_im)):
        high, low = split(value)
        ref[index, 2 * place * size : (2 * place + 1) * size] = high
        ref[index, (2 * place + 1) * size : (2 * place + 2) * size] = low


def dot_nn(a, b):
    return lax.dot_general(a, b, (((1,), (0,)), ((), ())), preferred_element_type=F32)


def dot_nt(a, b):
    return lax.dot_general(a, b, (((1,), (1,)), ((), ())), preferred_element_type=F32)


def three(stack, place, source, dot):
    high, low = source
    size = high.shape[0]
    both = stack[2 * place * size : (2 * place + 2) * size]
    wide = dot(both, high)
    return wide[:size] + wide[size:] + dot(both[:size], low)


def forms(source, full):
    if not full:
        return (split(source),)
    turned = source.T
    return split(source), split(source + turned), split(source - turned)


def products(stack, source):
    if len(source) == 1:
        return -three(stack, 0, source[0], dot_nt), three(stack, 0, source[0], dot_nn)
    shared = three(stack, 2, source[0], dot_nn)
    return shared - three(stack, 0, source[1], dot_nn), shared - three(stack, 1, source[2], dot_nn)


def role(axis):
    return role_of(lax.axis_index(axis))


def by_type(lower, body):
    @pl.when(lower)
    def _():
        body(True)

    @pl.when(jnp.logical_not(lower))
    def _():
        body(False)


def convert_kernel(state_hbm, occ_hbm, up_hbm, low_hbm, first, second, state, occ, up, low, sems):
    copies = [
        pltpu.make_async_copy(src, dst, sems.at[index])
        for index, (src, dst) in enumerate(((state_hbm, state), (occ_hbm, occ), (up_hbm, up), (low_hbm, low)))
    ]
    for copy in copies:
        copy.start()
    for copy in copies:
        copy.wait()
    slot = lax.axis_index("aux") & 1
    re, im = state[0, 0], state[0, 1]
    size = re.shape[0]
    total, diff = re + im, re - im
    herm = 0.5 * (total + diff.T)
    anti = 0.5 * (total.T - diff)
    first[0:size] = jnp.where(slot == 0, herm, anti)
    second[0:size] = jnp.where(slot == 0, anti, herm)
    lane = lax.broadcasted_iota(jnp.int32, (META, size), 1)
    modes = occ.shape[1]
    row = jnp.zeros((META, size), F32)
    for mode in range(modes):
        for place, table in enumerate((occ, up, low)):
            row = jnp.where(lane == place * modes + mode, table[0, mode].astype(F32), row)
    first[size : size + META] = row
    second[size : size + META] = row


def prepare_kernel(h_static, drive_op, couple, bath_coef, damping, h_a, h_b, h_c, q_out, damp_out):
    h_re = (h_static[0] + h_static[0].T) * 0.5
    h_im = (h_static[1] - h_static[1].T) * 0.5
    v_re = (drive_op[0] + drive_op[0].T) * 0.5
    v_im = (drive_op[1] - drive_op[1].T) * 0.5
    for h_out, moment in ((h_a, 0.0), (h_b, time_step / 2), (h_c, time_step)):
        drive = drive_amp * math.cos(drive_freq * moment)
        store_stack(h_out, 0, h_re + drive * v_re, h_im + drive * v_im)
    for mode in range(couple.shape[0]):
        q = (couple[mode] + couple[mode].T) * 0.5
        q_out[3 * mode] = q
        q_out[3 * mode + 1] = bath_coef[0, mode] * q
        q_out[3 * mode + 2] = bath_coef[1, mode] * q
        damp_out[mode] = jnp.full(damp_out.shape[1:], damping[mode], F32)


def arrive_kernel(which, array, q_ref, damp, h_ref, *refs):
    weights, base, rate, early = refs[-4:]
    problem, block, pair = role("aux")
    part = pair ^ problem ^ which
    size = q_ref.shape[1]
    modes = damp.shape[0]
    meta = array[size : size + 1]

    def entry(place, mode):
        column = place * modes + mode
        return meta[:, column : column + 1]

    total = jnp.zeros((1, 1), F32)
    for mode in range(modes):
        total = total + entry(0, mode) * damp[mode][0:1, 0:1]
    rate[part] = jnp.broadcast_to(total, rate.shape[1:])
    value = array[0:size]
    base[part] = value
    m, p = products(h_ref.at[0], forms(value, True))
    early[part] = m - total * value + p.T

    near = 4 * block + 3 * pair
    inward = 1 - 2 * pair
    twin = near + (1 - part) * inward
    last = jnp.where(part == 0, near + 2 * inward, near + 3 * inward)
    third = jnp.where(part == 0, near - 2 * inward, near + 2 * inward)
    for kind, source in enumerate((twin, near - inward, third, last)):
        source = jnp.where(source < 0, -9, source).astype(F32)
        w_re = jnp.zeros((size, size), F32)
        w_im = jnp.zeros((size, size), F32)
        for mode in range(modes):
            up = jnp.where(entry(1, mode) == source, 1.0, 0.0)
            down = jnp.where(entry(2, mode) == source, entry(0, mode), 0.0)
            w_re = w_re + (up * q_ref[3 * mode] + down * q_ref[3 * mode + 1])
            w_im = w_im + down * q_ref[3 * mode + 2]
        store_stack(weights, 4 * part + kind, w_re, w_im)


N_OWN, N_LINK_N, N_LINK_F, N_PARTNER_F, F_OWN, F_LINK_N, F_PARTNER_F, F_PARTNER_N = range(8)


def term(weights, row, source):
    m, p = products(weights.at[row], source)
    return m + p.T


def cross_kernel(base, weights, early, near_out, far_out):
    _, _, pair = role("aux")

    def body(lower):
        near_out[...] = early[0] + term(weights, N_OWN, forms(base[1], lower))
        far_out[...] = early[1] + term(weights, F_OWN, forms(base[0], not lower))

    by_type(pair == 1, body)


def own_kernel(near, far, h_ref, weights, rate, near_out, far_out):
    _, _, pair = role("aux")
    x_n, x_f = near[...], far[...]
    f_n, f_f = forms(x_n, True), forms(x_f, True)
    m_n, p_n = products(h_ref.at[0], f_n)
    m_f, p_f = products(h_ref.at[0], f_f)
    m_n = m_n - rate[0][0:1, 0:1] * x_n
    m_f = m_f - rate[1][0:1, 0:1] * x_f

    def body(lower):
        m_nf, p_nf = products(weights.at[N_OWN], f_f if lower else f_f[:1])
        m_fn, p_fn = products(weights.at[F_OWN], f_n[:1] if lower else f_n)
        near_out[...] = m_n + m_nf + (p_n + p_nf).T
        far_out[...] = m_f + m_fn + (p_f + p_fn).T

    by_type(pair == 1, body)


def pick(one, two, pair, sorted_already):
    if sorted_already:
        return one[...], two[...]
    problem, _, _ = role("aux")
    size = one.shape[1]
    near_first = pair == problem
    one, two = one[0:size], two[0:size]
    return jnp.where(near_first, one, two), jnp.where(near_first, two, one)


def partner_kernel(sorted_already, one, two, weights, near, far, near_out, far_out):
    _, _, pair = role("aux")
    x_n, x_f = pick(one, two, 1 - pair, sorted_already)

    def body(lower):
        f_n, f_f = forms(x_n, lower), forms(x_f, lower)
        near_out[...] = near[...] + term(weights, N_PARTNER_F, f_f)
        m_a, p_a = products(weights.at[F_PARTNER_F], f_f)
        m_b, p_b = products(weights.at[F_PARTNER_N], f_n)
        far_out[...] = far[...] + m_a + m_b + (p_a + p_b).T

    by_type(pair == 1, body)


def part_kernel(row, source, weights, early, out):
    _, _, pair = role("aux")

    def body(lower):
        out[...] = early[...] + term(weights, row, forms(source[...], lower))

    by_type(pair == 0, body)


def finish_kernel(row, part, step, weight, source, weights, early, base, acc, out, acc_out):
    _, _, pair = role("aux")

    def body(lower):
        slope = early[...] + term(weights, row, forms(source[...], lower))
        out[...] = base[part] + step * slope
        acc_out[...] = (acc[part] if len(acc.shape) == 3 else acc[...]) + weight * slope

    by_type(pair == 0, body)


def first_near_kernel(step, weight, one, two, weights, early, base, out, acc_out):
    _, _, pair = role("aux")
    x_n, x_f = pick(one, two, 1 - pair, False)

    def body(lower):
        m_a, p_a = products(weights.at[N_LINK_N], forms(x_n, lower))
        m_b, p_b = products(weights.at[N_LINK_F], forms(x_f, lower))
        slope = early[...] + m_a + m_b + (p_a + p_b).T
        out[...] = base[0] + step * slope
        acc_out[...] = base[0] + weight * slope

    by_type(pair == 0, body)


def first_far_kernel(step, weight, one, two, weights, early, base, out, acc_out):
    _, _, pair = role("aux")
    x_n, _ = pick(one, two, 1 - pair, False)

    def body(lower):
        slope = early[...] + term(weights, F_LINK_N, forms(x_n, lower))
        out[...] = base[1] + step * slope
        acc_out[...] = base[1] + weight * slope

    by_type(pair == 0, body)


def last_far_kernel(weight, source, weights, early, acc, out):
    _, _, pair = role("aux")

    def body(lower):
        out[...] = acc[...] + weight * (early[...] + term(weights, F_LINK_N, forms(source[...], lower)))

    by_type(pair == 0, body)


def last_near_kernel(weight, source, weights, early, acc, far, first, second):
    problem, _, pair = role("aux")
    near_first = pair == problem

    def body(lower):
        near = acc[...] + weight * (early[...] + term(weights, N_LINK_F, forms(source[...], lower)))
        first[...] = jnp.where(near_first, near, far[...])
        second[...] = jnp.where(near_first, far[...], near)

    by_type(pair == 0, body)


def restore_kernel(first, second, first_sent, second_sent, out):
    device = lax.axis_index("aux")
    slot = device & 1
    keep_first, keep_second = kept(device)
    one = jnp.where(keep_first, first_sent[...], first[...])
    two = jnp.where(keep_second, second_sent[...], second[...])
    herm = jnp.where(slot == 0, one, two)
    anti = jnp.where(slot == 0, two, one)
    total = herm + anti.T
    diff = herm.T - anti
    out[0, 0] = 0.5 * (total + diff)
    out[0, 1] = 0.5 * (total - diff)


def call(kernel, out_shapes, args, smem=(), flops=0, space=None, scratch=(), grant=32, aliases=None):
    shapes = [jax.ShapeDtypeStruct(shape, dtype) for shape, dtype in out_shapes]
    moved = sum(math.prod(a.shape) * a.dtype.itemsize for a in list(args) + shapes)
    single = len(shapes) == 1
    return pl.pallas_call(
        kernel,
        out_shape=shapes[0] if single else shapes,
        in_specs=[space or (SMEM if index in smem else VMEM) for index in range(len(args))],
        out_specs=VMEM if single else [VMEM] * len(shapes),
        scratch_shapes=scratch,
        input_output_aliases=aliases or {},
        cost_estimate=pl.CostEstimate(flops=flops, bytes_accessed=moved, transcendentals=0),
        compiler_params=pltpu.CompilerParams(vmem_limit_bytes=grant * 1024 * 1024),
    )(*args)


def on_device(state, h_static, drive_op, couple, bath_coef, damping, occupation, raise_nbr, lower_nbr):
    count = lax.axis_size("aux")
    size = state.shape[-1]
    modes = couple.shape[0]
    first_to, second_to, link_to, core_to = permutations(count)
    pair_shape = (2, size, size)
    unit = 2 * size**3

    def send(value, pairs):
        return lax.ppermute(value, "aux", pairs)

    tall = ((size + META, size), F32)
    tables = [occupation, raise_nbr, lower_nbr]
    first, second = call(
        convert_kernel,
        [tall, tall],
        [state] + tables,
        space=pl.BlockSpec(memory_space=pltpu.HBM),
        grant=60,
        scratch=[pltpu.VMEM(state.shape, F32)]
        + [pltpu.SMEM(table.shape, jnp.int32) for table in tables]
        + [pltpu.SemaphoreType.DMA((4,))],
    )
    keep_first, keep_second = kept(lax.axis_index("aux"))
    first = jnp.where(keep_first, first, send(first, first_to))
    second = jnp.where(keep_second, second, send(second, second_to))
    *h_now, q_all, damp = call(
        prepare_kernel,
        [((1, 6 * size, size), BF16)] * 3 + [((3 * modes, size, size), F32), ((modes, 8, 128), F32)],
        [h_static, drive_op, couple, bath_coef, damping],
        smem=(3, 4),
    )
    flat = ((size, size), F32)

    held = [((8, 6 * size, size), BF16), (pair_shape, F32), ((2, 8, 128), F32), (pair_shape, F32)]
    state_now = call(partial(arrive_kernel, 0), held, [first, q_all, damp, h_now[0]], flops=9 * unit)
    link = [send(first, link_to)]
    partner = [send(first, core_to)]
    weights, base, rate, early = call(
        partial(arrive_kernel, 1),
        held,
        [second, q_all, damp, h_now[0], *state_now],
        flops=9 * unit,
        aliases={4 + index: index for index in range(4)},
    )
    link.append(send(second, link_to))
    partner.append(send(second, core_to))
    near_e, far_e = call(cross_kernel, [flat, flat], [base, weights, early], flops=15 * unit)
    steps = (time_step / 2, time_step / 2, time_step)
    shares = (time_step / 6, time_step / 3, time_step / 3, time_step / 6)

    def with_partner(stage, near_e, far_e):
        return call(
            partial(partner_kernel, stage > 0), [flat, flat], [*partner, weights, near_e, far_e], flops=27 * unit
        )

    def own(stage, near, far):
        args = [near, far, h_now[(0, 1, 1, 2)[stage]], weights, rate]
        return call(own_kernel, [flat, flat], args, flops=33 * unit)

    def part(row, source, early):
        return call(partial(part_kernel, row), [flat], [source, weights, early], flops=9 * unit)

    def finish(stage, row, which, source, early, acc):
        return call(
            partial(finish_kernel, row, which, steps[stage], shares[stage]),
            [flat, flat],
            [source, weights, early, base, acc],
            flops=9 * unit,
        )

    near_e, far_e = with_partner(0, near_e, far_e)
    near, near_acc = call(
        partial(first_near_kernel, steps[0], shares[0]), [flat, flat], [*link, weights, near_e, base], flops=18 * unit
    )
    far, far_acc = call(
        partial(first_far_kernel, steps[0], shares[0]), [flat, flat], [*link, weights, far_e, base], flops=9 * unit
    )
    link_n, link_f = send(near, link_to), send(far, link_to)
    partner = [send(near, core_to), send(far, core_to)]
    near_e, far_e = with_partner(1, *own(1, near, far))
    far, far_acc = finish(1, F_LINK_N, 1, link_n, far_e, far_acc)
    next_f = send(far, link_to)
    near_e = part(N_LINK_N, link_n, near_e)
    near, near_acc = finish(1, N_LINK_F, 0, link_f, near_e, near_acc)
    link_n, link_f = send(near, link_to), next_f
    partner = [send(near, core_to), send(far, core_to)]
    near_e, far_e = with_partner(2, *own(2, near, far))
    near_e = part(N_LINK_F, link_f, near_e)
    near, near_acc = finish(2, N_LINK_N, 0, link_n, near_e, near_acc)
    far, far_acc = finish(2, F_LINK_N, 1, link_n, far_e, far_acc)
    link_n, link_f = send(near, link_to), send(far, link_to)
    partner = [send(near, core_to), send(far, core_to)]
    near_e, far_e = with_partner(3, *own(3, near, far))
    far = call(partial(last_far_kernel, shares[3]), [flat], [link_n, weights, far_e, far_acc], flops=9 * unit)
    near_e = part(N_LINK_N, link_n, near_e)
    first, second = call(
        partial(last_near_kernel, shares[3]), [flat, flat], [link_f, weights, near_e, near_acc, far], flops=9 * unit
    )
    back = [send(first, flipped(first_to)), send(second, flipped(second_to)), first, second]
    return call(restore_kernel, [((1, 2, size, size), F32)], back)


def solution(mesh):
    return jax.shard_map(
        on_device,
        mesh=mesh,
        in_specs=(
            P("aux", None, None, None),
            P(),
            P(),
            P(),
            P(),
            P(),
            P("aux", None),
            P("aux", None),
            P("aux", None),
        ),
        out_specs=P("aux", None, None, None),
        check_vma=False,
    )
```

```python
import math
from functools import partial

import jax
import jax.numpy as jnp
from jax import lax
from jax.experimental import pallas as pl
from jax.experimental.pallas import tpu as pltpu
from jax.sharding import PartitionSpec as P


time_step = 0.05
drive_amp = 2.0
drive_freq = 20.0
META = 8
CHUNK = 32
F32 = jnp.float32
BF16 = jnp.bfloat16
VMEM = pl.BlockSpec(memory_space=pltpu.VMEM)
SMEM = pl.BlockSpec(memory_space=pltpu.SMEM)


def chip_of(problem, block):
    group, odd = block >> 1, block & 1
    return group * 4 + problem * 2 + (odd ^ (group & 1))


def device_of(problem, block, pair):
    return chip_of(problem, block) * 2 + ((block & 1) ^ pair)


def role_of(device):
    core, x, problem, group = device & 1, (device >> 1) & 1, (device >> 2) & 1, device >> 3
    odd = x ^ (group & 1)
    return problem, 2 * group + odd, core ^ odd


def permutations(count):
    blocks = count // 4
    first, second, link = [], [], []
    for device in range(count):
        block, half, slot = device >> 2, (device >> 1) & 1, device & 1
        first.append((device, device_of(slot, block, half)))
        second.append((device, device_of(1 - slot, block, half)))
    for problem in range(2):
        for block in range(blocks - 1):
            here, there = device_of(problem, block, 1), device_of(problem, block + 1, 0)
            link += [(here, there), (there, here)]
    for block, pair in ((0, 0), (blocks - 1, 1)):
        here, there = device_of(0, block, pair), device_of(1, block, pair)
        link += [(here, there), (there, here)]
    core = [(device, device ^ 1) for device in range(count)]
    return full(first), full(second), sorted(link), core


def full(pairs):
    fixed = [a for a, b in pairs if a == b]
    swaps = dict(zip(fixed[::2], fixed[1::2]))
    swaps.update({b: a for a, b in swaps.items()})
    return [(a, swaps.get(a, b)) for a, b in pairs]


def kept(device):
    block, half, slot = device >> 2, (device >> 1) & 1, device & 1
    return device_of(slot, block, half) == device, device_of(1 - slot, block, half) == device


def flipped(pairs):
    return sorted((b, a) for a, b in pairs)


def split(value):
    high = value.astype(BF16)
    return high, (value - high.astype(F32)).astype(BF16)


def store_stack(ref, index, w_re, w_im=None):
    size = w_re.shape[0]
    for place, value in enumerate((w_re,) if w_im is None else (w_re, w_im, w_re + w_im)):
        high, low = split(value)
        ref[index, 2 * place * size : (2 * place + 1) * size] = high
        ref[index, (2 * place + 1) * size : (2 * place + 2) * size] = low


def store_rows(ref, index, row, size, values):
    for place, value in enumerate(values):
        high, low = split(value)
        start = 2 * place * size + row
        ref[index, start : start + value.shape[0]] = high
        ref[index, start + size : start + size + value.shape[0]] = low


def dot_nn(a, b):
    return lax.dot_general(a, b, (((1,), (0,)), ((), ())), preferred_element_type=F32)


def dot_nt(a, b):
    return lax.dot_general(a, b, (((1,), (1,)), ((), ())), preferred_element_type=F32)


def three(stack, place, source, dot):
    high, low = source
    size = high.shape[0]
    both = stack[2 * place * size : (2 * place + 2) * size]
    wide = dot(both, high)
    return wide[:size] + wide[size:] + dot(both[:size], low)


def forms(source, full):
    if not full:
        return (split(source),)
    turned = source.T
    return split(source), split(source + turned), split(source - turned)


def products(stack, source):
    if len(source) == 1:
        return -three(stack, 0, source[0], dot_nt), three(stack, 0, source[0], dot_nn)
    shared = three(stack, 2, source[0], dot_nn)
    return shared - three(stack, 0, source[1], dot_nn), shared - three(stack, 1, source[2], dot_nn)


def role(axis):
    return role_of(lax.axis_index(axis))


def by_type(lower, body):
    @pl.when(lower)
    def _():
        body(True)

    @pl.when(jnp.logical_not(lower))
    def _():
        body(False)


def convert_kernel(state_hbm, occ_hbm, up_hbm, low_hbm, first, second, state, occ, up, low, sems):
    copies = [
        pltpu.make_async_copy(src, dst, sems.at[index])
        for index, (src, dst) in enumerate(((state_hbm, state), (occ_hbm, occ), (up_hbm, up), (low_hbm, low)))
    ]
    for copy in copies:
        copy.start()
    for copy in copies:
        copy.wait()
    slot = lax.axis_index("aux") & 1
    re, im = state[0, 0], state[0, 1]
    size = re.shape[0]
    total, diff = re + im, re - im
    herm = 0.5 * (total + diff.T)
    anti = 0.5 * (total.T - diff)
    first[0:size] = jnp.where(slot == 0, herm, anti)
    second[0:size] = jnp.where(slot == 0, anti, herm)
    lane = lax.broadcasted_iota(jnp.int32, (META, size), 1)
    modes = occ.shape[1]
    row = jnp.zeros((META, size), F32)
    for mode in range(modes):
        for place, table in enumerate((occ, up, low)):
            row = jnp.where(lane == place * modes + mode, table[0, mode].astype(F32), row)
    first[size : size + META] = row
    second[size : size + META] = row


def prepare_kernel(h_static, drive_op, couple, bath_coef, damping, h_a, h_b, h_c, q_out, damp_out):
    h_re = (h_static[0] + h_static[0].T) * 0.5
    h_im = (h_static[1] - h_static[1].T) * 0.5
    v_re = (drive_op[0] + drive_op[0].T) * 0.5
    v_im = (drive_op[1] - drive_op[1].T) * 0.5
    for h_out, moment in ((h_a, 0.0), (h_b, time_step / 2), (h_c, time_step)):
        drive = drive_amp * math.cos(drive_freq * moment)
        store_stack(h_out, 0, h_re + drive * v_re, h_im + drive * v_im)
    for mode in range(couple.shape[0]):
        q_out[mode] = (couple[mode] + couple[mode].T) * 0.5
        for place, value in enumerate((damping[mode], bath_coef[0, mode], bath_coef[1, mode])):
            damp_out[3 * mode + place] = jnp.full(damp_out.shape[1:], value, F32)


def arrive_kernel(which, array, q_ref, damp, h_ref, *refs):
    weights, base, rate, early = refs[-4:]
    problem, block, pair = role("aux")
    part = pair ^ problem ^ which
    size = q_ref.shape[1]
    modes = q_ref.shape[0]
    meta = array[size : size + 1]

    def entry(place, mode):
        column = place * modes + mode
        return meta[:, column : column + 1]

    def constant(place, mode):
        return damp[3 * mode + place][0:1, 0:1]

    total = jnp.zeros((1, 1), F32)
    for mode in range(modes):
        total = total + entry(0, mode) * constant(0, mode)
    rate[part] = jnp.broadcast_to(total, rate.shape[1:])
    value = array[0:size]
    base[part] = value
    m, p = products(h_ref.at[0], forms(value, True))
    early[part] = m - total * value + p.T

    near = 4 * block + 3 * pair
    inward = 1 - 2 * pair
    from_below = pair == 0
    sources = (
        jnp.where(part == 0, near + inward, near),
        near - inward,
        jnp.where(part == 0, near - 2 * inward, near + 2 * inward),
        jnp.where(part == 0, near + 2 * inward, near + 3 * inward),
    )
    link_kinds = (1 - part, 2 - part)
    partner_kinds = (2 * part, 3)
    link_sources = (jnp.where(part == 0, sources[1], sources[0]), jnp.where(part == 0, sources[2], sources[1]))
    partner_sources = (jnp.where(part == 0, sources[0], sources[2]), sources[3])

    def marked(place, source, mode):
        return entry(place, mode) == jnp.where(source < 0, -9, source).astype(F32)

    for index in range(2):
        kind = jnp.where(from_below, link_kinds[index], partner_kinds[index])
        source = jnp.where(from_below, link_sources[index], partner_sources[index])
        factors = []
        for mode in range(modes):
            down = jnp.where(marked(2, source, mode), entry(0, mode), 0.0)
            factors.append((down * constant(1, mode), down * constant(2, mode)))
        for row in range(0, size, CHUNK):
            w_re = sum(factors[mode][0] * q_ref[mode, row : row + CHUNK] for mode in range(modes))
            w_im = sum(factors[mode][1] * q_ref[mode, row : row + CHUNK] for mode in range(modes))
            store_rows(weights, 4 * part + kind, row, size, (w_re, w_im, w_re + w_im))
    for index in range(2):
        kind = jnp.where(from_below, partner_kinds[index], link_kinds[index])
        source = jnp.where(from_below, partner_sources[index], link_sources[index])
        factors = [jnp.where(marked(1, source, mode), 1.0, 0.0) for mode in range(modes)]
        for row in range(0, size, CHUNK):
            w_re = sum(factors[mode] * q_ref[mode, row : row + CHUNK] for mode in range(modes))
            store_rows(weights, 4 * part + kind, row, size, (w_re,))


N_OWN, N_LINK_N, N_LINK_F, N_PARTNER_F, F_OWN, F_LINK_N, F_PARTNER_F, F_PARTNER_N = range(8)


def term(weights, row, source):
    m, p = products(weights.at[row], source)
    return m + p.T


def cross_kernel(base, weights, early, near_out, far_out):
    _, _, pair = role("aux")

    def body(lower):
        near_out[...] = early[0] + term(weights, N_OWN, forms(base[1], lower))
        far_out[...] = early[1] + term(weights, F_OWN, forms(base[0], not lower))

    by_type(pair == 1, body)


def own_kernel(near, far, h_ref, weights, rate, near_out, far_out):
    _, _, pair = role("aux")
    x_n, x_f = near[...], far[...]
    f_n, f_f = forms(x_n, True), forms(x_f, True)
    m_n, p_n = products(h_ref.at[0], f_n)
    m_f, p_f = products(h_ref.at[0], f_f)
    m_n = m_n - rate[0][0:1, 0:1] * x_n
    m_f = m_f - rate[1][0:1, 0:1] * x_f

    def body(lower):
        m_nf, p_nf = products(weights.at[N_OWN], f_f if lower else f_f[:1])
        m_fn, p_fn = products(weights.at[F_OWN], f_n[:1] if lower else f_n)
        near_out[...] = m_n + m_nf + (p_n + p_nf).T
        far_out[...] = m_f + m_fn + (p_f + p_fn).T

    by_type(pair == 1, body)


def pick(one, two, pair, sorted_already):
    if sorted_already:
        return one[...], two[...]
    problem, _, _ = role("aux")
    size = one.shape[1]
    near_first = pair == problem
    one, two = one[0:size], two[0:size]
    return jnp.where(near_first, one, two), jnp.where(near_first, two, one)


def partner_kernel(sorted_already, one, two, weights, near, far, near_out, far_out):
    _, _, pair = role("aux")
    x_n, x_f = pick(one, two, 1 - pair, sorted_already)

    def body(lower):
        f_n, f_f = forms(x_n, lower), forms(x_f, lower)
        near_out[...] = near[...] + term(weights, N_PARTNER_F, f_f)
        m_a, p_a = products(weights.at[F_PARTNER_F], f_f)
        m_b, p_b = products(weights.at[F_PARTNER_N], f_n)
        far_out[...] = far[...] + m_a + m_b + (p_a + p_b).T

    by_type(pair == 1, body)


def part_kernel(row, source, weights, early, out):
    _, _, pair = role("aux")

    def body(lower):
        out[...] = early[...] + term(weights, row, forms(source[...], lower))

    by_type(pair == 0, body)


def finish_kernel(row, part, step, weight, source, weights, early, base, acc, out, acc_out):
    _, _, pair = role("aux")

    def body(lower):
        slope = early[...] + term(weights, row, forms(source[...], lower))
        out[...] = base[part] + step * slope
        acc_out[...] = (acc[part] if len(acc.shape) == 3 else acc[...]) + weight * slope

    by_type(pair == 0, body)


def first_near_kernel(step, weight, one, two, weights, early, base, out, acc_out):
    _, _, pair = role("aux")
    x_n, x_f = pick(one, two, 1 - pair, False)

    def body(lower):
        m_a, p_a = products(weights.at[N_LINK_N], forms(x_n, lower))
        m_b, p_b = products(weights.at[N_LINK_F], forms(x_f, lower))
        slope = early[...] + m_a + m_b + (p_a + p_b).T
        out[...] = base[0] + step * slope
        acc_out[...] = base[0] + weight * slope

    by_type(pair == 0, body)


def first_far_kernel(step, weight, one, two, weights, early, base, out, acc_out):
    _, _, pair = role("aux")
    x_n, _ = pick(one, two, 1 - pair, False)

    def body(lower):
        slope = early[...] + term(weights, F_LINK_N, forms(x_n, lower))
        out[...] = base[1] + step * slope
        acc_out[...] = base[1] + weight * slope

    by_type(pair == 0, body)


def last_far_kernel(weight, source, weights, early, acc, out):
    _, _, pair = role("aux")

    def body(lower):
        out[...] = acc[...] + weight * (early[...] + term(weights, F_LINK_N, forms(source[...], lower)))

    by_type(pair == 0, body)


def last_near_kernel(weight, source, weights, early, acc, far, first, second):
    problem, _, pair = role("aux")
    near_first = pair == problem

    def body(lower):
        near = acc[...] + weight * (early[...] + term(weights, N_LINK_F, forms(source[...], lower)))
        first[...] = jnp.where(near_first, near, far[...])
        second[...] = jnp.where(near_first, far[...], near)

    by_type(pair == 0, body)


def restore_kernel(first, second, first_sent, second_sent, out):
    device = lax.axis_index("aux")
    slot = device & 1
    keep_first, keep_second = kept(device)
    one = jnp.where(keep_first, first_sent[...], first[...])
    two = jnp.where(keep_second, second_sent[...], second[...])
    herm = jnp.where(slot == 0, one, two)
    anti = jnp.where(slot == 0, two, one)
    total = herm + anti.T
    diff = herm.T - anti
    out[0, 0] = 0.5 * (total + diff)
    out[0, 1] = 0.5 * (total - diff)


def call(kernel, out_shapes, args, smem=(), flops=0, space=None, scratch=(), grant=32, aliases=None):
    shapes = [jax.ShapeDtypeStruct(shape, dtype) for shape, dtype in out_shapes]
    moved = sum(math.prod(a.shape) * a.dtype.itemsize for a in list(args) + shapes)
    single = len(shapes) == 1
    return pl.pallas_call(
        kernel,
        out_shape=shapes[0] if single else shapes,
        in_specs=[space or (SMEM if index in smem else VMEM) for index in range(len(args))],
        out_specs=VMEM if single else [VMEM] * len(shapes),
        scratch_shapes=scratch,
        input_output_aliases=aliases or {},
        cost_estimate=pl.CostEstimate(flops=flops, bytes_accessed=moved, transcendentals=0),
        compiler_params=pltpu.CompilerParams(vmem_limit_bytes=grant * 1024 * 1024),
    )(*args)


def on_device(state, h_static, drive_op, couple, bath_coef, damping, occupation, raise_nbr, lower_nbr):
    count = lax.axis_size("aux")
    size = state.shape[-1]
    modes = couple.shape[0]
    first_to, second_to, link_to, core_to = permutations(count)
    pair_shape = (2, size, size)
    unit = 2 * size**3

    def send(value, pairs):
        return lax.ppermute(value, "aux", pairs)

    tall = ((size + META, size), F32)
    tables = [occupation, raise_nbr, lower_nbr]
    first, second = call(
        convert_kernel,
        [tall, tall],
        [state] + tables,
        space=pl.BlockSpec(memory_space=pltpu.HBM),
        grant=60,
        scratch=[pltpu.VMEM(state.shape, F32)]
        + [pltpu.SMEM(table.shape, jnp.int32) for table in tables]
        + [pltpu.SemaphoreType.DMA((4,))],
    )
    keep_first, keep_second = kept(lax.axis_index("aux"))
    first = jnp.where(keep_first, first, send(first, first_to))
    second = jnp.where(keep_second, second, send(second, second_to))
    *h_now, q_all, damp = call(
        prepare_kernel,
        [((1, 6 * size, size), BF16)] * 3 + [((modes, size, size), F32), ((3 * modes, 8, 128), F32)],
        [h_static, drive_op, couple, bath_coef, damping],
        smem=(3, 4),
    )
    flat = ((size, size), F32)

    held = [((8, 6 * size, size), BF16), (pair_shape, F32), ((2, 8, 128), F32), (pair_shape, F32)]
    state_now = call(partial(arrive_kernel, 0), held, [first, q_all, damp, h_now[0]], flops=9 * unit)
    link = [send(first, link_to)]
    partner = [send(first, core_to)]
    weights, base, rate, early = call(
        partial(arrive_kernel, 1),
        held,
        [second, q_all, damp, h_now[0], *state_now],
        flops=9 * unit,
        aliases={4 + index: index for index in range(4)},
    )
    link.append(send(second, link_to))
    partner.append(send(second, core_to))
    near_e, far_e = call(cross_kernel, [flat, flat], [base, weights, early], flops=15 * unit)
    steps = (time_step / 2, time_step / 2, time_step)
    shares = (time_step / 6, time_step / 3, time_step / 3, time_step / 6)

    def with_partner(stage, near_e, far_e):
        return call(
            partial(partner_kernel, stage > 0), [flat, flat], [*partner, weights, near_e, far_e], flops=27 * unit
        )

    def own(stage, near, far):
        args = [near, far, h_now[(0, 1, 1, 2)[stage]], weights, rate]
        return call(own_kernel, [flat, flat], args, flops=33 * unit)

    def part(row, source, early):
        return call(partial(part_kernel, row), [flat], [source, weights, early], flops=9 * unit)

    def finish(stage, row, which, source, early, acc):
        return call(
            partial(finish_kernel, row, which, steps[stage], shares[stage]),
            [flat, flat],
            [source, weights, early, base, acc],
            flops=9 * unit,
        )

    near_e, far_e = with_partner(0, near_e, far_e)
    near, near_acc = call(
        partial(first_near_kernel, steps[0], shares[0]), [flat, flat], [*link, weights, near_e, base], flops=18 * unit
    )
    far, far_acc = call(
        partial(first_far_kernel, steps[0], shares[0]), [flat, flat], [*link, weights, far_e, base], flops=9 * unit
    )
    link_n, link_f = send(near, link_to), send(far, link_to)
    partner = [send(near, core_to), send(far, core_to)]
    near_e, far_e = with_partner(1, *own(1, near, far))
    far, far_acc = finish(1, F_LINK_N, 1, link_n, far_e, far_acc)
    next_f = send(far, link_to)
    near_e = part(N_LINK_N, link_n, near_e)
    near, near_acc = finish(1, N_LINK_F, 0, link_f, near_e, near_acc)
    link_n, link_f = send(near, link_to), next_f
    partner = [send(near, core_to), send(far, core_to)]
    near_e, far_e = with_partner(2, *own(2, near, far))
    near_e = part(N_LINK_F, link_f, near_e)
    near, near_acc = finish(2, N_LINK_N, 0, link_n, near_e, near_acc)
    far, far_acc = finish(2, F_LINK_N, 1, link_n, far_e, far_acc)
    link_n, link_f = send(near, link_to), send(far, link_to)
    partner = [send(near, core_to), send(far, core_to)]
    near_e, far_e = with_partner(3, *own(3, near, far))
    far = call(partial(last_far_kernel, shares[3]), [flat], [link_n, weights, far_e, far_acc], flops=9 * unit)
    near_e = part(N_LINK_N, link_n, near_e)
    first, second = call(
        partial(last_near_kernel, shares[3]), [flat, flat], [link_f, weights, near_e, near_acc, far], flops=9 * unit
    )
    back = [send(first, flipped(first_to)), send(second, flipped(second_to)), first, second]
    return call(restore_kernel, [((1, 2, size, size), F32)], back)


def solution(mesh):
    return jax.shard_map(
        on_device,
        mesh=mesh,
        in_specs=(
            P("aux", None, None, None),
            P(),
            P(),
            P(),
            P(),
            P(),
            P("aux", None),
            P("aux", None),
            P("aux", None),
        ),
        out_specs=P("aux", None, None, None),
        check_vma=False,
    )
```

```python
import math
from functools import partial

import jax
import jax.numpy as jnp
from jax import lax
from jax.experimental import pallas as pl
from jax.experimental.pallas import tpu as pltpu
from jax.sharding import PartitionSpec as P


time_step = 0.05
drive_amp = 2.0
drive_freq = 20.0
META = 8
CHUNK = 32
F32 = jnp.float32
BF16 = jnp.bfloat16
VMEM = pl.BlockSpec(memory_space=pltpu.VMEM)
SMEM = pl.BlockSpec(memory_space=pltpu.SMEM)


def chip_of(problem, block):
    group, odd = block >> 1, block & 1
    return group * 4 + problem * 2 + (odd ^ (group & 1))


def device_of(problem, block, pair):
    return chip_of(problem, block) * 2 + ((block & 1) ^ pair)


def role_of(device):
    core, x, problem, group = device & 1, (device >> 1) & 1, (device >> 2) & 1, device >> 3
    odd = x ^ (group & 1)
    return problem, 2 * group + odd, core ^ odd


def permutations(count):
    blocks = count // 4
    first, second, link = [], [], []
    for device in range(count):
        block, half, slot = device >> 2, (device >> 1) & 1, device & 1
        first.append((device, device_of(slot, block, half)))
        second.append((device, device_of(1 - slot, block, half)))
    for problem in range(2):
        for block in range(blocks - 1):
            here, there = device_of(problem, block, 1), device_of(problem, block + 1, 0)
            link += [(here, there), (there, here)]
    for block, pair in ((0, 0), (blocks - 1, 1)):
        here, there = device_of(0, block, pair), device_of(1, block, pair)
        link += [(here, there), (there, here)]
    core = [(device, device ^ 1) for device in range(count)]
    return full(first), full(second), sorted(link), core


def full(pairs):
    fixed = [a for a, b in pairs if a == b]
    swaps = {}
    for place in range(0, len(fixed) - 3, 4):
        for a, b in ((fixed[place], fixed[place + 2]), (fixed[place + 1], fixed[place + 3])):
            swaps.update({a: b, b: a})
    return [(a, swaps.get(a, b)) for a, b in pairs]


def kept(device):
    block, half, slot = device >> 2, (device >> 1) & 1, device & 1
    return device_of(slot, block, half) == device, device_of(1 - slot, block, half) == device


def flipped(pairs):
    return sorted((b, a) for a, b in pairs)


def split(value):
    high = value.astype(BF16)
    return high, (value - high.astype(F32)).astype(BF16)


def store_stack(ref, index, w_re, w_im=None):
    size = w_re.shape[0]
    for place, value in enumerate((w_re,) if w_im is None else (w_re, w_im, w_re + w_im)):
        high, low = split(value)
        ref[index, 2 * place * size : (2 * place + 1) * size] = high
        ref[index, (2 * place + 1) * size : (2 * place + 2) * size] = low


def store_rows(ref, index, row, size, values):
    for place, value in enumerate(values):
        high, low = split(value)
        start = 2 * place * size + row
        ref[index, start : start + value.shape[0]] = high
        ref[index, start + size : start + size + value.shape[0]] = low


def dot_nn(a, b):
    return lax.dot_general(a, b, (((1,), (0,)), ((), ())), preferred_element_type=F32)


def dot_nt(a, b):
    return lax.dot_general(a, b, (((1,), (1,)), ((), ())), preferred_element_type=F32)


def three(stack, place, source, dot):
    high, low = source
    size = high.shape[0]
    both = stack[2 * place * size : (2 * place + 2) * size]
    wide = dot(both, high)
    return wide[:size] + wide[size:] + dot(both[:size], low)


def forms(source, full):
    if not full:
        return (split(source),)
    turned = source.T
    return split(source), split(source + turned), split(source - turned)


def products(stack, source):
    if len(source) == 1:
        return -three(stack, 0, source[0], dot_nt), three(stack, 0, source[0], dot_nn)
    shared = three(stack, 2, source[0], dot_nn)
    return shared - three(stack, 0, source[1], dot_nn), shared - three(stack, 1, source[2], dot_nn)


def role(axis):
    return role_of(lax.axis_index(axis))


def by_type(lower, body):
    @pl.when(lower)
    def _():
        body(True)

    @pl.when(jnp.logical_not(lower))
    def _():
        body(False)


def convert_kernel(state_hbm, occ_hbm, up_hbm, low_hbm, first, second, state, occ, up, low, sems):
    copies = [
        pltpu.make_async_copy(src, dst, sems.at[index])
        for index, (src, dst) in enumerate(((state_hbm, state), (occ_hbm, occ), (up_hbm, up), (low_hbm, low)))
    ]
    for copy in copies:
        copy.start()
    for copy in copies:
        copy.wait()
    slot = lax.axis_index("aux") & 1
    re, im = state[0, 0], state[0, 1]
    size = re.shape[0]
    total, diff = re + im, re - im
    herm = 0.5 * (total + diff.T)
    anti = 0.5 * (total.T - diff)
    first[0:size] = jnp.where(slot == 0, herm, anti)
    second[0:size] = jnp.where(slot == 0, anti, herm)
    lane = lax.broadcasted_iota(jnp.int32, (META, size), 1)
    modes = occ.shape[1]
    row = jnp.zeros((META, size), F32)
    for mode in range(modes):
        for place, table in enumerate((occ, up, low)):
            row = jnp.where(lane == place * modes + mode, table[0, mode].astype(F32), row)
    first[size : size + META] = row
    second[size : size + META] = row


def prepare_kernel(h_static, drive_op, couple, bath_coef, damping, h_a, h_b, h_c, q_out, damp_out):
    h_re = (h_static[0] + h_static[0].T) * 0.5
    h_im = (h_static[1] - h_static[1].T) * 0.5
    v_re = (drive_op[0] + drive_op[0].T) * 0.5
    v_im = (drive_op[1] - drive_op[1].T) * 0.5
    for h_out, moment in ((h_a, 0.0), (h_b, time_step / 2), (h_c, time_step)):
        drive = drive_amp * math.cos(drive_freq * moment)
        store_stack(h_out, 0, h_re + drive * v_re, h_im + drive * v_im)
    for mode in range(couple.shape[0]):
        q_out[mode] = (couple[mode] + couple[mode].T) * 0.5
        for place, value in enumerate((damping[mode], bath_coef[0, mode], bath_coef[1, mode])):
            damp_out[3 * mode + place] = jnp.full(damp_out.shape[1:], value, F32)


def arrive_kernel(which, array, q_ref, damp, h_ref, *refs):
    weights, base, rate, early = refs[-4:]
    problem, block, pair = role("aux")
    part = pair ^ problem ^ which
    size = q_ref.shape[1]
    modes = q_ref.shape[0]
    meta = array[size : size + 1]

    def entry(place, mode):
        column = place * modes + mode
        return meta[:, column : column + 1]

    def constant(place, mode):
        return damp[3 * mode + place][0:1, 0:1]

    total = jnp.zeros((1, 1), F32)
    for mode in range(modes):
        total = total + entry(0, mode) * constant(0, mode)
    rate[part] = jnp.broadcast_to(total, rate.shape[1:])
    value = array[0:size]
    base[part] = value
    m, p = products(h_ref.at[0], forms(value, True))
    early[part] = m - total * value + p.T

    near = 4 * block + 3 * pair
    inward = 1 - 2 * pair
    from_below = pair == 0
    sources = (
        jnp.where(part == 0, near + inward, near),
        near - inward,
        jnp.where(part == 0, near - 2 * inward, near + 2 * inward),
        jnp.where(part == 0, near + 2 * inward, near + 3 * inward),
    )
    link_kinds = (1 - part, 2 - part)
    partner_kinds = (2 * part, 3)
    link_sources = (jnp.where(part == 0, sources[1], sources[0]), jnp.where(part == 0, sources[2], sources[1]))
    partner_sources = (jnp.where(part == 0, sources[0], sources[2]), sources[3])

    def marked(place, source, mode):
        return entry(place, mode) == jnp.where(source < 0, -9, source).astype(F32)

    for index in range(2):
        kind = jnp.where(from_below, link_kinds[index], partner_kinds[index])
        source = jnp.where(from_below, link_sources[index], partner_sources[index])
        factors = []
        for mode in range(modes):
            down = jnp.where(marked(2, source, mode), entry(0, mode), 0.0)
            factors.append((down * constant(1, mode), down * constant(2, mode)))
        for row in range(0, size, CHUNK):
            w_re = sum(factors[mode][0] * q_ref[mode, row : row + CHUNK] for mode in range(modes))
            w_im = sum(factors[mode][1] * q_ref[mode, row : row + CHUNK] for mode in range(modes))
            store_rows(weights, 4 * part + kind, row, size, (w_re, w_im, w_re + w_im))
    for index in range(2):
        kind = jnp.where(from_below, partner_kinds[index], link_kinds[index])
        source = jnp.where(from_below, partner_sources[index], link_sources[index])
        factors = [jnp.where(marked(1, source, mode), 1.0, 0.0) for mode in range(modes)]
        for row in range(0, size, CHUNK):
            w_re = sum(factors[mode] * q_ref[mode, row : row + CHUNK] for mode in range(modes))
            store_rows(weights, 4 * part + kind, row, size, (w_re,))


N_OWN, N_LINK_N, N_LINK_F, N_PARTNER_F, F_OWN, F_LINK_N, F_PARTNER_F, F_PARTNER_N = range(8)


def term(weights, row, source):
    m, p = products(weights.at[row], source)
    return m + p.T


def cross_kernel(base, weights, early, near_out, far_out):
    _, _, pair = role("aux")

    def body(lower):
        near_out[...] = early[0] + term(weights, N_OWN, forms(base[1], lower))
        far_out[...] = early[1] + term(weights, F_OWN, forms(base[0], not lower))

    by_type(pair == 1, body)


def own_kernel(near, far, h_ref, weights, rate, near_out, far_out):
    _, _, pair = role("aux")
    x_n, x_f = near[...], far[...]
    f_n, f_f = forms(x_n, True), forms(x_f, True)
    m_n, p_n = products(h_ref.at[0], f_n)
    m_f, p_f = products(h_ref.at[0], f_f)
    m_n = m_n - rate[0][0:1, 0:1] * x_n
    m_f = m_f - rate[1][0:1, 0:1] * x_f

    def body(lower):
        m_nf, p_nf = products(weights.at[N_OWN], f_f if lower else f_f[:1])
        m_fn, p_fn = products(weights.at[F_OWN], f_n[:1] if lower else f_n)
        near_out[...] = m_n + m_nf + (p_n + p_nf).T
        far_out[...] = m_f + m_fn + (p_f + p_fn).T

    by_type(pair == 1, body)


def pick(one, two, pair, sorted_already):
    if sorted_already:
        return one[...], two[...]
    problem, _, _ = role("aux")
    size = one.shape[1]
    near_first = pair == problem
    one, two = one[0:size], two[0:size]
    return jnp.where(near_first, one, two), jnp.where(near_first, two, one)


def partner_kernel(sorted_already, one, two, weights, near, far, near_out, far_out):
    _, _, pair = role("aux")
    x_n, x_f = pick(one, two, 1 - pair, sorted_already)

    def body(lower):
        f_n, f_f = forms(x_n, lower), forms(x_f, lower)
        near_out[...] = near[...] + term(weights, N_PARTNER_F, f_f)
        m_a, p_a = products(weights.at[F_PARTNER_F], f_f)
        m_b, p_b = products(weights.at[F_PARTNER_N], f_n)
        far_out[...] = far[...] + m_a + m_b + (p_a + p_b).T

    by_type(pair == 1, body)


def part_kernel(row, source, weights, early, out):
    _, _, pair = role("aux")

    def body(lower):
        out[...] = early[...] + term(weights, row, forms(source[...], lower))

    by_type(pair == 0, body)


def finish_kernel(row, part, step, weight, source, weights, early, base, acc, out, acc_out):
    _, _, pair = role("aux")

    def body(lower):
        slope = early[...] + term(weights, row, forms(source[...], lower))
        out[...] = base[part] + step * slope
        acc_out[...] = (acc[part] if len(acc.shape) == 3 else acc[...]) + weight * slope

    by_type(pair == 0, body)


def first_near_kernel(step, weight, one, two, weights, early, base, out, acc_out):
    _, _, pair = role("aux")
    x_n, x_f = pick(one, two, 1 - pair, False)

    def body(lower):
        m_a, p_a = products(weights.at[N_LINK_N], forms(x_n, lower))
        m_b, p_b = products(weights.at[N_LINK_F], forms(x_f, lower))
        slope = early[...] + m_a + m_b + (p_a + p_b).T
        out[...] = base[0] + step * slope
        acc_out[...] = base[0] + weight * slope

    by_type(pair == 0, body)


def first_far_kernel(step, weight, one, two, weights, early, base, out, acc_out):
    _, _, pair = role("aux")
    x_n, _ = pick(one, two, 1 - pair, False)

    def body(lower):
        slope = early[...] + term(weights, F_LINK_N, forms(x_n, lower))
        out[...] = base[1] + step * slope
        acc_out[...] = base[1] + weight * slope

    by_type(pair == 0, body)


def last_far_kernel(weight, source, weights, early, acc, out):
    _, _, pair = role("aux")

    def body(lower):
        out[...] = acc[...] + weight * (early[...] + term(weights, F_LINK_N, forms(source[...], lower)))

    by_type(pair == 0, body)


def last_near_kernel(weight, source, weights, early, acc, far, first, second):
    problem, _, pair = role("aux")
    near_first = pair == problem

    def body(lower):
        near = acc[...] + weight * (early[...] + term(weights, N_LINK_F, forms(source[...], lower)))
        first[...] = jnp.where(near_first, near, far[...])
        second[...] = jnp.where(near_first, far[...], near)

    by_type(pair == 0, body)


def restore_kernel(first, second, first_sent, second_sent, out):
    device = lax.axis_index("aux")
    slot = device & 1
    keep_first, keep_second = kept(device)
    one = jnp.where(keep_first, first_sent[...], first[...])
    two = jnp.where(keep_second, second_sent[...], second[...])
    herm = jnp.where(slot == 0, one, two)
    anti = jnp.where(slot == 0, two, one)
    total = herm + anti.T
    diff = herm.T - anti
    out[0, 0] = 0.5 * (total + diff)
    out[0, 1] = 0.5 * (total - diff)


def call(kernel, out_shapes, args, smem=(), flops=0, space=None, scratch=(), grant=32, aliases=None):
    shapes = [jax.ShapeDtypeStruct(shape, dtype) for shape, dtype in out_shapes]
    moved = sum(math.prod(a.shape) * a.dtype.itemsize for a in list(args) + shapes)
    single = len(shapes) == 1
    return pl.pallas_call(
        kernel,
        out_shape=shapes[0] if single else shapes,
        in_specs=[space or (SMEM if index in smem else VMEM) for index in range(len(args))],
        out_specs=VMEM if single else [VMEM] * len(shapes),
        scratch_shapes=scratch,
        input_output_aliases=aliases or {},
        cost_estimate=pl.CostEstimate(flops=flops, bytes_accessed=moved, transcendentals=0),
        compiler_params=pltpu.CompilerParams(vmem_limit_bytes=grant * 1024 * 1024),
    )(*args)


def on_device(state, h_static, drive_op, couple, bath_coef, damping, occupation, raise_nbr, lower_nbr):
    count = lax.axis_size("aux")
    size = state.shape[-1]
    modes = couple.shape[0]
    first_to, second_to, link_to, core_to = permutations(count)
    pair_shape = (2, size, size)
    unit = 2 * size**3

    def send(value, pairs):
        return lax.ppermute(value, "aux", pairs)

    tall = ((size + META, size), F32)
    tables = [occupation, raise_nbr, lower_nbr]
    first, second = call(
        convert_kernel,
        [tall, tall],
        [state] + tables,
        space=pl.BlockSpec(memory_space=pltpu.HBM),
        grant=60,
        scratch=[pltpu.VMEM(state.shape, F32)]
        + [pltpu.SMEM(table.shape, jnp.int32) for table in tables]
        + [pltpu.SemaphoreType.DMA((4,))],
    )
    keep_first, keep_second = kept(lax.axis_index("aux"))
    first = jnp.where(keep_first, first, send(first, first_to))
    second = jnp.where(keep_second, second, send(second, second_to))
    *h_now, q_all, damp = call(
        prepare_kernel,
        [((1, 6 * size, size), BF16)] * 3 + [((modes, size, size), F32), ((3 * modes, 8, 128), F32)],
        [h_static, drive_op, couple, bath_coef, damping],
        smem=(3, 4),
    )
    flat = ((size, size), F32)

    held = [((8, 6 * size, size), BF16), (pair_shape, F32), ((2, 8, 128), F32), (pair_shape, F32)]
    state_now = call(partial(arrive_kernel, 0), held, [first, q_all, damp, h_now[0]], flops=9 * unit)
    link = [send(first, link_to)]
    partner = [send(first, core_to)]
    weights, base, rate, early = call(
        partial(arrive_kernel, 1),
        held,
        [second, q_all, damp, h_now[0], *state_now],
        flops=9 * unit,
        aliases={4 + index: index for index in range(4)},
    )
    link.append(send(second, link_to))
    partner.append(send(second, core_to))
    near_e, far_e = call(cross_kernel, [flat, flat], [base, weights, early], flops=15 * unit)
    steps = (time_step / 2, time_step / 2, time_step)
    shares = (time_step / 6, time_step / 3, time_step / 3, time_step / 6)

    def with_partner(stage, near_e, far_e):
        return call(
            partial(partner_kernel, stage > 0), [flat, flat], [*partner, weights, near_e, far_e], flops=27 * unit
        )

    def own(stage, near, far):
        args = [near, far, h_now[(0, 1, 1, 2)[stage]], weights, rate]
        return call(own_kernel, [flat, flat], args, flops=33 * unit)

    def part(row, source, early):
        return call(partial(part_kernel, row), [flat], [source, weights, early], flops=9 * unit)

    def finish(stage, row, which, source, early, acc):
        return call(
            partial(finish_kernel, row, which, steps[stage], shares[stage]),
            [flat, flat],
            [source, weights, early, base, acc],
            flops=9 * unit,
        )

    near_e, far_e = with_partner(0, near_e, far_e)
    near, near_acc = call(
        partial(first_near_kernel, steps[0], shares[0]), [flat, flat], [*link, weights, near_e, base], flops=18 * unit
    )
    far, far_acc = call(
        partial(first_far_kernel, steps[0], shares[0]), [flat, flat], [*link, weights, far_e, base], flops=9 * unit
    )
    link_n, link_f = send(near, link_to), send(far, link_to)
    partner = [send(near, core_to), send(far, core_to)]
    near_e, far_e = with_partner(1, *own(1, near, far))
    far, far_acc = finish(1, F_LINK_N, 1, link_n, far_e, far_acc)
    next_f = send(far, link_to)
    near_e = part(N_LINK_N, link_n, near_e)
    near, near_acc = finish(1, N_LINK_F, 0, link_f, near_e, near_acc)
    link_n, link_f = send(near, link_to), next_f
    partner = [send(near, core_to), send(far, core_to)]
    near_e, far_e = with_partner(2, *own(2, near, far))
    near_e = part(N_LINK_F, link_f, near_e)
    near, near_acc = finish(2, N_LINK_N, 0, link_n, near_e, near_acc)
    far, far_acc = finish(2, F_LINK_N, 1, link_n, far_e, far_acc)
    link_n, link_f = send(near, link_to), send(far, link_to)
    partner = [send(near, core_to), send(far, core_to)]
    near_e, far_e = with_partner(3, *own(3, near, far))
    far = call(partial(last_far_kernel, shares[3]), [flat], [link_n, weights, far_e, far_acc], flops=9 * unit)
    near_e = part(N_LINK_N, link_n, near_e)
    first, second = call(
        partial(last_near_kernel, shares[3]), [flat, flat], [link_f, weights, near_e, near_acc, far], flops=9 * unit
    )
    back = [send(first, flipped(first_to)), send(second, flipped(second_to)), first, second]
    return call(restore_kernel, [((1, 2, size, size), F32)], back)


def solution(mesh):
    return jax.shard_map(
        on_device,
        mesh=mesh,
        in_specs=(
            P("aux", None, None, None),
            P(),
            P(),
            P(),
            P(),
            P(),
            P("aux", None),
            P("aux", None),
            P("aux", None),
        ),
        out_specs=P("aux", None, None, None),
        check_vma=False,
    )
```

```python
import math
from functools import partial

import jax
import jax.numpy as jnp
from jax import lax
from jax.experimental import pallas as pl
from jax.experimental.pallas import tpu as pltpu
from jax.sharding import PartitionSpec as P


time_step = 0.05
drive_amp = 2.0
drive_freq = 20.0
META = 8
CHUNK = 32
F32 = jnp.float32
BF16 = jnp.bfloat16
VMEM = pl.BlockSpec(memory_space=pltpu.VMEM)
SMEM = pl.BlockSpec(memory_space=pltpu.SMEM)


def chip_of(problem, block):
    group, odd = block >> 1, block & 1
    return group * 4 + problem * 2 + (odd ^ (group & 1))


def device_of(problem, block, pair):
    return chip_of(problem, block) * 2 + ((block & 1) ^ pair)


def role_of(device):
    core, x, problem, group = device & 1, (device >> 1) & 1, (device >> 2) & 1, device >> 3
    odd = x ^ (group & 1)
    return problem, 2 * group + odd, core ^ odd


def start_of(device):
    return device >> 2, (device >> 1) & 1, device & 1, (device >> 3) & 1


def targets_of(device):
    block, half, slot, _ = start_of(device)
    problem = slot ^ half
    return device_of(problem ^ 1, block, half), device_of(problem, block, half)


def straight(device):
    block, half, _, parity = start_of(device)
    return half == ((block & 1) ^ parity)


def permutations(count):
    blocks = count // 4
    first, second, rows, columns, link = [], [], [], [], []
    for device in range(count):
        block, half, slot, parity = start_of(device)
        to_first, to_second = targets_of(device)
        first.append((device, to_first))
        second.append((device, to_second))
        idle = device ^ 8 if device ^ 8 < count else device
        rows.append((device, device ^ 5 if (slot ^ half) != (block & 1) else idle))
        idle = device ^ 9 if device ^ 9 < count else device
        columns.append((device, device ^ 2 if slot != parity else idle))
    for problem in range(2):
        for block in range(blocks - 1):
            here, there = device_of(problem, block, 1), device_of(problem, block + 1, 0)
            link += [(here, there), (there, here)]
    for block, pair in ((0, 0), (blocks - 1, 1)):
        here, there = device_of(0, block, pair), device_of(1, block, pair)
        link += [(here, there), (there, here)]
    core = [(device, device ^ 1) for device in range(count)]
    return full(first), full(second), rows, columns, sorted(link), core


def full(pairs):
    fixed = [a for a, b in pairs if a == b]
    swaps = {}
    for place in range(0, len(fixed) - 3, 4):
        for a, b in ((fixed[place], fixed[place + 2]), (fixed[place + 1], fixed[place + 3])):
            swaps.update({a: b, b: a})
    return [(a, swaps.get(a, b)) for a, b in pairs]


def kept(device):
    first, second = targets_of(device)
    return first == device, second == device


def flipped(pairs):
    return sorted((b, a) for a, b in pairs)


def split(value):
    high = value.astype(BF16)
    return high, (value - high.astype(F32)).astype(BF16)


def store_stack(ref, index, w_re, w_im=None):
    size = w_re.shape[0]
    for place, value in enumerate((w_re,) if w_im is None else (w_re, w_im, w_re + w_im)):
        high, low = split(value)
        ref[index, 2 * place * size : (2 * place + 1) * size] = high
        ref[index, (2 * place + 1) * size : (2 * place + 2) * size] = low


def store_rows(ref, index, row, size, values):
    for place, value in enumerate(values):
        high, low = split(value)
        start = 2 * place * size + row
        ref[index, start : start + value.shape[0]] = high
        ref[index, start + size : start + size + value.shape[0]] = low


def dot_nn(a, b):
    return lax.dot_general(a, b, (((1,), (0,)), ((), ())), preferred_element_type=F32)


def dot_nt(a, b):
    return lax.dot_general(a, b, (((1,), (1,)), ((), ())), preferred_element_type=F32)


def three(stack, place, source, dot):
    high, low = source
    size = high.shape[0]
    both = stack[2 * place * size : (2 * place + 2) * size]
    wide = dot(both, high)
    return wide[:size] + wide[size:] + dot(both[:size], low)


def forms(source, full):
    if not full:
        return (split(source),)
    turned = source.T
    return split(source), split(source + turned), split(source - turned)


def products(stack, source):
    if len(source) == 1:
        return -three(stack, 0, source[0], dot_nt), three(stack, 0, source[0], dot_nn)
    shared = three(stack, 2, source[0], dot_nn)
    return shared - three(stack, 0, source[1], dot_nn), shared - three(stack, 1, source[2], dot_nn)


def role(axis):
    return role_of(lax.axis_index(axis))


def by_type(lower, body):
    @pl.when(lower)
    def _():
        body(True)

    @pl.when(jnp.logical_not(lower))
    def _():
        body(False)


def convert_kernel(which, *refs):
    inputs, out, held, sems = refs[:6], refs[6], refs[7:13], refs[13]
    state, occ, up, low, bath, damp = held
    copies = [
        pltpu.make_async_copy(src, dst, sems.at[index]) for index, (src, dst) in enumerate(zip(inputs, held))
    ]
    for copy in copies:
        copy.start()
    for copy in copies:
        copy.wait()
    _, half, slot, _ = start_of(lax.axis_index("aux"))
    problem = slot ^ half ^ 1 ^ which
    re, im = state[0, 0], state[0, 1]
    size = re.shape[0]

    @pl.when(problem == 0)
    def _():
        out[0:size] = 0.5 * ((re + im) + (re - im).T)

    @pl.when(problem == 1)
    def _():
        out[0:size] = 0.5 * ((re + im).T - (re - im))

    lane = lax.broadcasted_iota(jnp.int32, (META, size), 1)
    modes = occ.shape[1]
    row = jnp.zeros((META, size), F32)
    for mode in range(modes):
        for place, table in enumerate((occ, up, low)):
            row = jnp.where(lane == place * modes + mode, table[0, mode].astype(F32), row)
        for place, value in enumerate((damp[mode], bath[0, mode], bath[1, mode])):
            row = jnp.where(lane == (3 + place) * modes + mode, value, row)
    out[size : size + META] = row


def prepare_kernel(h_static, drive_op, couple, h_a, h_b, h_c, q_out):
    h_re = (h_static[0] + h_static[0].T) * 0.5
    h_im = (h_static[1] - h_static[1].T) * 0.5
    v_re = (drive_op[0] + drive_op[0].T) * 0.5
    v_im = (drive_op[1] - drive_op[1].T) * 0.5
    for h_out, moment in ((h_a, 0.0), (h_b, time_step / 2), (h_c, time_step)):
        drive = drive_amp * math.cos(drive_freq * moment)
        store_stack(h_out, 0, h_re + drive * v_re, h_im + drive * v_im)
    for mode in range(couple.shape[0]):
        q_out[mode] = (couple[mode] + couple[mode].T) * 0.5


def arrive_kernel(which, array, q_ref, h_ref, *refs):
    weights, base, rate, early = refs[-4:]
    problem, block, pair = role("aux")
    part = problem ^ 1 ^ which
    size = q_ref.shape[1]
    modes = q_ref.shape[0]
    meta = array[size : size + 1]

    def entry(place, mode):
        column = place * modes + mode
        return meta[:, column : column + 1]

    def constant(place, mode):
        return entry(3 + place, mode)

    total = jnp.zeros((1, 1), F32)
    for mode in range(modes):
        total = total + entry(0, mode) * constant(0, mode)
    rate[part] = jnp.broadcast_to(total, rate.shape[1:])
    value = array[0:size]
    base[part] = value
    m, p = products(h_ref.at[0], forms(value, True))
    early[part] = m - total * value + p.T

    near = 4 * block + 3 * pair
    inward = 1 - 2 * pair
    from_below = pair == 0
    sources = (
        jnp.where(part == 0, near + inward, near),
        near - inward,
        jnp.where(part == 0, near - 2 * inward, near + 2 * inward),
        jnp.where(part == 0, near + 2 * inward, near + 3 * inward),
    )
    link_kinds = (1 - part, 2 - part)
    partner_kinds = (2 * part, 3)
    link_sources = (jnp.where(part == 0, sources[1], sources[0]), jnp.where(part == 0, sources[2], sources[1]))
    partner_sources = (jnp.where(part == 0, sources[0], sources[2]), sources[3])

    def marked(place, source, mode):
        return entry(place, mode) == jnp.where(source < 0, -9, source).astype(F32)

    for index in range(2):
        kind = jnp.where(from_below, link_kinds[index], partner_kinds[index])
        source = jnp.where(from_below, link_sources[index], partner_sources[index])
        factors = []
        for mode in range(modes):
            down = jnp.where(marked(2, source, mode), entry(0, mode), 0.0)
            factors.append((down * constant(1, mode), down * constant(2, mode)))
        for row in range(0, size, CHUNK):
            w_re = sum(factors[mode][0] * q_ref[mode, row : row + CHUNK] for mode in range(modes))
            w_im = sum(factors[mode][1] * q_ref[mode, row : row + CHUNK] for mode in range(modes))
            store_rows(weights, 4 * part + kind, row, size, (w_re, w_im, w_re + w_im))
    for index in range(2):
        kind = jnp.where(from_below, partner_kinds[index], link_kinds[index])
        source = jnp.where(from_below, partner_sources[index], link_sources[index])
        factors = [jnp.where(marked(1, source, mode), 1.0, 0.0) for mode in range(modes)]
        for row in range(0, size, CHUNK):
            w_re = sum(factors[mode] * q_ref[mode, row : row + CHUNK] for mode in range(modes))
            store_rows(weights, 4 * part + kind, row, size, (w_re,))


N_OWN, N_LINK_N, N_LINK_F, N_PARTNER_F, F_OWN, F_LINK_N, F_PARTNER_F, F_PARTNER_N = range(8)


def term(weights, row, source):
    m, p = products(weights.at[row], source)
    return m + p.T


def cross_kernel(base, weights, early, near_out, far_out):
    _, _, pair = role("aux")

    def body(lower):
        near_out[...] = early[0] + term(weights, N_OWN, forms(base[1], lower))
        far_out[...] = early[1] + term(weights, F_OWN, forms(base[0], not lower))

    by_type(pair == 1, body)


def own_kernel(near, far, h_ref, weights, rate, near_out, far_out):
    _, _, pair = role("aux")
    x_n, x_f = near[...], far[...]
    f_n, f_f = forms(x_n, True), forms(x_f, True)
    m_n, p_n = products(h_ref.at[0], f_n)
    m_f, p_f = products(h_ref.at[0], f_f)
    m_n = m_n - rate[0][0:1, 0:1] * x_n
    m_f = m_f - rate[1][0:1, 0:1] * x_f

    def body(lower):
        m_nf, p_nf = products(weights.at[N_OWN], f_f if lower else f_f[:1])
        m_fn, p_fn = products(weights.at[F_OWN], f_n[:1] if lower else f_n)
        near_out[...] = m_n + m_nf + (p_n + p_nf).T
        far_out[...] = m_f + m_fn + (p_f + p_fn).T

    by_type(pair == 1, body)


def pick(one, two, sorted_already):
    if sorted_already:
        return one[...], two[...]
    problem, _, _ = role("aux")
    size = one.shape[1]
    near_first = problem == 1
    one, two = one[0:size], two[0:size]
    return jnp.where(near_first, one, two), jnp.where(near_first, two, one)


def partner_kernel(sorted_already, one, two, weights, near, far, near_out, far_out):
    _, _, pair = role("aux")
    x_n, x_f = pick(one, two, sorted_already)

    def body(lower):
        f_n, f_f = forms(x_n, lower), forms(x_f, lower)
        near_out[...] = near[...] + term(weights, N_PARTNER_F, f_f)
        m_a, p_a = products(weights.at[F_PARTNER_F], f_f)
        m_b, p_b = products(weights.at[F_PARTNER_N], f_n)
        far_out[...] = far[...] + m_a + m_b + (p_a + p_b).T

    by_type(pair == 1, body)


def part_kernel(row, source, weights, early, out):
    _, _, pair = role("aux")

    def body(lower):
        out[...] = early[...] + term(weights, row, forms(source[...], lower))

    by_type(pair == 0, body)


def finish_kernel(row, part, step, weight, source, weights, early, base, acc, out, acc_out):
    _, _, pair = role("aux")

    def body(lower):
        slope = early[...] + term(weights, row, forms(source[...], lower))
        out[...] = base[part] + step * slope
        acc_out[...] = (acc[part] if len(acc.shape) == 3 else acc[...]) + weight * slope

    by_type(pair == 0, body)


def sent_far(which):
    problem, _, _ = role("aux")
    return problem ^ 1 ^ which


def first_part_kernel(array, weights, near, far, near_out, far_out):
    _, _, pair = role("aux")
    is_far = sent_far(0)

    def body(lower):
        source = forms(array[0 : array.shape[1]], lower)
        near_out[...] = near[...] + term(weights, N_LINK_N + is_far, source)

        @pl.when(is_far == 0)
        def _():
            far_out[...] = far[...] + term(weights, F_LINK_N, source)

        @pl.when(is_far == 1)
        def _():
            far_out[...] = far[...]

    by_type(pair == 0, body)


def first_near_kernel(step, weight, array, weights, early, base, out, acc_out):
    _, _, pair = role("aux")

    def body(lower):
        source = forms(array[0 : array.shape[1]], lower)
        slope = early[...] + term(weights, N_LINK_N + sent_far(1), source)
        out[...] = base[0] + step * slope
        acc_out[...] = base[0] + weight * slope

    by_type(pair == 0, body)


def first_far_kernel(step, weight, array, weights, early, base, out, acc_out):
    _, _, pair = role("aux")
    is_far = sent_far(1)

    def store(slope):
        out[...] = base[1] + step * slope
        acc_out[...] = base[1] + weight * slope

    def body(lower):
        @pl.when(is_far == 0)
        def _():
            store(early[...] + term(weights, F_LINK_N, forms(array[0 : array.shape[1]], lower)))

    by_type(pair == 0, body)

    @pl.when(is_far == 1)
    def _():
        store(early[...])


def last_far_kernel(weight, source, weights, early, acc, out):
    _, _, pair = role("aux")

    def body(lower):
        out[...] = acc[...] + weight * (early[...] + term(weights, F_LINK_N, forms(source[...], lower)))

    by_type(pair == 0, body)


def last_near_kernel(weight, source, weights, early, acc, far, first, second):
    problem, _, pair = role("aux")
    near_first = problem == 1

    def body(lower):
        near = acc[...] + weight * (early[...] + term(weights, N_LINK_F, forms(source[...], lower)))
        first[...] = jnp.where(near_first, near, far[...])
        second[...] = jnp.where(near_first, far[...], near)

    by_type(pair == 0, body)


def restore_kernel(first, second, first_sent, second_sent, out_hbm, out, sems):
    device = lax.axis_index("aux")
    _, half, slot, _ = start_of(device)
    keep_first, keep_second = kept(device)
    one = jnp.where(keep_first, first_sent[...], first[...])
    two = jnp.where(keep_second, second_sent[...], second[...])
    herm = jnp.where(slot == half, two, one)
    anti = jnp.where(slot == half, one, two)
    total = herm + anti.T
    diff = herm.T - anti
    copies = []
    for half, value in enumerate((total + diff, total - diff)):
        out[0, half] = 0.5 * value
        copies.append(pltpu.make_async_copy(out.at[0, half], out_hbm.at[0, half], sems.at[half]))
        copies[-1].start()
    for copy in copies:
        copy.wait()


def call(kernel, out_shapes, args, smem=(), flops=0, space=None, scratch=(), grant=32, aliases=None, out_space=None):
    shapes = [jax.ShapeDtypeStruct(shape, dtype) for shape, dtype in out_shapes]
    moved = sum(math.prod(a.shape) * a.dtype.itemsize for a in list(args) + shapes)
    single = len(shapes) == 1
    return pl.pallas_call(
        kernel,
        out_shape=shapes[0] if single else shapes,
        in_specs=[space or (SMEM if index in smem else VMEM) for index in range(len(args))],
        out_specs=(out_space or VMEM) if single else [VMEM] * len(shapes),
        scratch_shapes=scratch,
        input_output_aliases=aliases or {},
        cost_estimate=pl.CostEstimate(flops=flops, bytes_accessed=moved, transcendentals=0),
        compiler_params=pltpu.CompilerParams(vmem_limit_bytes=grant * 1024 * 1024),
    )(*args)


def on_device(state, h_static, drive_op, couple, bath_coef, damping, occupation, raise_nbr, lower_nbr):
    count = lax.axis_size("aux")
    size = state.shape[-1]
    modes = couple.shape[0]
    first_to, second_to, rows_to, columns_to, link_to, core_to = permutations(count)
    pair_shape = (2, size, size)
    unit = 2 * size**3

    def send(value, pairs):
        return lax.ppermute(value, "aux", pairs)

    tall = ((size + META, size), F32)
    tables = [occupation, raise_nbr, lower_nbr, bath_coef, damping]
    first, second = (
        call(
            partial(convert_kernel, which),
            [tall],
            [state] + tables,
            space=pl.BlockSpec(memory_space=pltpu.HBM),
            grant=60,
            scratch=[pltpu.VMEM(state.shape, F32)]
            + [pltpu.SMEM(table.shape, table.dtype) for table in tables]
            + [pltpu.SemaphoreType.DMA((1 + len(tables),))],
        )
        for which in range(2)
    )
    device = lax.axis_index("aux")
    _, _, slot, parity = start_of(device)
    keep_first, _ = kept(device)
    crossed = send(second, rows_to)
    first = jnp.where(keep_first, first, send(first, first_to))
    is_straight = straight(device)
    turned = send(jnp.where(is_straight, crossed, second), columns_to)
    second = jnp.where(slot == parity, jnp.where(is_straight, second, crossed), turned)
    *h_now, q_all = call(
        prepare_kernel, [((1, 6 * size, size), BF16)] * 3 + [((modes, size, size), F32)], [h_static, drive_op, couple]
    )
    flat = ((size, size), F32)

    held = [((8, 6 * size, size), BF16), (pair_shape, F32), ((2, 8, 128), F32), (pair_shape, F32)]
    state_now = call(partial(arrive_kernel, 0), held, [first, q_all, h_now[0]], flops=9 * unit)
    link = [send(first, link_to)]
    partner = [send(first, core_to)]
    weights, base, rate, early = call(
        partial(arrive_kernel, 1),
        held,
        [second, q_all, h_now[0], *state_now],
        flops=9 * unit,
        aliases={3 + index: index for index in range(4)},
    )
    link.append(send(second, link_to))
    partner.append(send(second, core_to))
    near_e, far_e = call(cross_kernel, [flat, flat], [base, weights, early], flops=15 * unit)
    steps = (time_step / 2, time_step / 2, time_step)
    shares = (time_step / 6, time_step / 3, time_step / 3, time_step / 6)

    def with_partner(stage, near_e, far_e):
        return call(
            partial(partner_kernel, stage > 0), [flat, flat], [*partner, weights, near_e, far_e], flops=27 * unit
        )

    def own(stage, near, far):
        args = [near, far, h_now[(0, 1, 1, 2)[stage]], weights, rate]
        return call(own_kernel, [flat, flat], args, flops=33 * unit)

    def part(row, source, early):
        return call(partial(part_kernel, row), [flat], [source, weights, early], flops=9 * unit)

    def finish(stage, row, which, source, early, acc):
        return call(
            partial(finish_kernel, row, which, steps[stage], shares[stage]),
            [flat, flat],
            [source, weights, early, base, acc],
            flops=9 * unit,
        )

    near_e, far_e = with_partner(0, near_e, far_e)
    near_e, far_e = call(first_part_kernel, [flat, flat], [link[0], weights, near_e, far_e], flops=18 * unit)
    near, near_acc = call(
        partial(first_near_kernel, steps[0], shares[0]), [flat, flat], [link[1], weights, near_e, base], flops=9 * unit
    )
    far, far_acc = call(
        partial(first_far_kernel, steps[0], shares[0]), [flat, flat], [link[1], weights, far_e, base], flops=9 * unit
    )
    link_n, link_f = send(near, link_to), send(far, link_to)
    partner = [send(near, core_to), send(far, core_to)]
    near_e, far_e = with_partner(1, *own(1, near, far))
    far, far_acc = finish(1, F_LINK_N, 1, link_n, far_e, far_acc)
    next_f = send(far, link_to)
    near_e = part(N_LINK_N, link_n, near_e)
    near, near_acc = finish(1, N_LINK_F, 0, link_f, near_e, near_acc)
    link_n, link_f = send(near, link_to), next_f
    partner = [send(near, core_to), send(far, core_to)]
    near_e, far_e = with_partner(2, *own(2, near, far))
    near_e = part(N_LINK_F, link_f, near_e)
    near, near_acc = finish(2, N_LINK_N, 0, link_n, near_e, near_acc)
    far, far_acc = finish(2, F_LINK_N, 1, link_n, far_e, far_acc)
    link_n, link_f = send(near, link_to), send(far, link_to)
    partner = [send(near, core_to), send(far, core_to)]
    near_e, far_e = with_partner(3, *own(3, near, far))
    far = call(partial(last_far_kernel, shares[3]), [flat], [link_n, weights, far_e, far_acc], flops=9 * unit)
    near_e = part(N_LINK_N, link_n, near_e)
    first, second = call(
        partial(last_near_kernel, shares[3]), [flat, flat], [link_f, weights, near_e, near_acc, far], flops=9 * unit
    )
    back = [send(first, flipped(first_to)), send(second, flipped(second_to)), first, second]
    return call(
        restore_kernel,
        [(state.shape, F32)],
        back,
        out_space=pl.BlockSpec(memory_space=pltpu.HBM),
        scratch=[pltpu.VMEM(state.shape, F32), pltpu.SemaphoreType.DMA((2,))],
    )


def solution(mesh):
    return jax.shard_map(
        on_device,
        mesh=mesh,
        in_specs=(
            P("aux", None, None, None),
            P(),
            P(),
            P(),
            P(),
            P(),
            P("aux", None),
            P("aux", None),
            P("aux", None),
        ),
        out_specs=P("aux", None, None, None),
        check_vma=False,
    )
```

```python
import math
from functools import partial

import jax
import jax.numpy as jnp
from jax import lax
from jax.experimental import pallas as pl
from jax.experimental.pallas import tpu as pltpu
from jax.sharding import PartitionSpec as P


time_step = 0.05
drive_amp = 2.0
drive_freq = 20.0
META = 8
CHUNK = 32
F32 = jnp.float32
BF16 = jnp.bfloat16
VMEM = pl.BlockSpec(memory_space=pltpu.VMEM)
SMEM = pl.BlockSpec(memory_space=pltpu.SMEM)


def chip_of(problem, block):
    group, odd = block >> 1, block & 1
    return group * 4 + problem * 2 + (odd ^ (group & 1))


def device_of(problem, block, pair):
    return chip_of(problem, block) * 2 + ((block & 1) ^ pair)


def role_of(device):
    core, x, problem, group = device & 1, (device >> 1) & 1, (device >> 2) & 1, device >> 3
    odd = x ^ (group & 1)
    return problem, 2 * group + odd, core ^ odd


def start_of(device):
    return device >> 2, (device >> 1) & 1, device & 1, (device >> 3) & 1


def targets_of(device):
    block, half, slot, _ = start_of(device)
    problem = slot ^ half
    return device_of(problem ^ 1, block, half), device_of(problem, block, half)


def homes_of(device):
    block, half, slot, _ = start_of(device)
    return device_of(slot, block, half), device_of(1 - slot, block, half)


def straight(device):
    block, half, _, parity = start_of(device)
    return half == ((block & 1) ^ parity)


def permutations(count):
    blocks = count // 4
    first, rows, columns, link = [], [], [], []
    back = [[(device, homes_of(device)[place]) for device in range(count)] for place in range(2)]
    for device in range(count):
        block, half, slot, parity = start_of(device)
        first.append((device, targets_of(device)[0]))
        idle = device ^ 8 if device ^ 8 < count else device
        rows.append((device, device ^ 5 if (slot ^ half) != (block & 1) else idle))
        idle = device ^ 9 if device ^ 9 < count else device
        columns.append((device, device ^ 2 if slot != parity else idle))
    for problem in range(2):
        for block in range(blocks - 1):
            here, there = device_of(problem, block, 1), device_of(problem, block + 1, 0)
            link += [(here, there), (there, here)]
    for block, pair in ((0, 0), (blocks - 1, 1)):
        here, there = device_of(0, block, pair), device_of(1, block, pair)
        link += [(here, there), (there, here)]
    core = [(device, device ^ 1) for device in range(count)]
    back = [flipped(full(pairs)) for pairs in back]
    return full(first), rows, columns, sorted(link), core, back


def full(pairs):
    fixed = [a for a, b in pairs if a == b]
    swaps = {}
    for place in range(0, len(fixed) - 3, 4):
        for a, b in ((fixed[place], fixed[place + 2]), (fixed[place + 1], fixed[place + 3])):
            swaps.update({a: b, b: a})
    return [(a, swaps.get(a, b)) for a, b in pairs]


def kept(device):
    first, second = homes_of(device)
    return first == device, second == device


def flipped(pairs):
    return sorted((b, a) for a, b in pairs)


def split(value):
    high = value.astype(BF16)
    return high, (value - high.astype(F32)).astype(BF16)


def store_stack(ref, index, w_re, w_im=None):
    size = w_re.shape[0]
    for place, value in enumerate((w_re,) if w_im is None else (w_re, w_im, w_re + w_im)):
        high, low = split(value)
        ref[index, 2 * place * size : (2 * place + 1) * size] = high
        ref[index, (2 * place + 1) * size : (2 * place + 2) * size] = low


def store_rows(ref, index, row, size, values):
    for place, value in enumerate(values):
        high, low = split(value)
        start = 2 * place * size + row
        ref[index, start : start + value.shape[0]] = high
        ref[index, start + size : start + size + value.shape[0]] = low


def dot_nn(a, b):
    return lax.dot_general(a, b, (((1,), (0,)), ((), ())), preferred_element_type=F32)


def dot_nt(a, b):
    return lax.dot_general(a, b, (((1,), (1,)), ((), ())), preferred_element_type=F32)


def three(stack, place, source, dot):
    high, low = source
    size = high.shape[0]
    both = stack[2 * place * size : (2 * place + 2) * size]
    wide = dot(both, high)
    return wide[:size] + wide[size:] + dot(both[:size], low)


def forms(source, full):
    if not full:
        return (split(source),)
    turned = source.T
    return split(source), split(source + turned), split(source - turned)


def products(stack, source):
    if len(source) == 1:
        return -three(stack, 0, source[0], dot_nt), three(stack, 0, source[0], dot_nn)
    shared = three(stack, 2, source[0], dot_nn)
    return shared - three(stack, 0, source[1], dot_nn), shared - three(stack, 1, source[2], dot_nn)


def role(axis):
    return role_of(lax.axis_index(axis))


def by_type(lower, body):
    @pl.when(lower)
    def _():
        body(True)

    @pl.when(jnp.logical_not(lower))
    def _():
        body(False)


def convert_kernel(which, *refs):
    inputs, out, held, sems = refs[:6], refs[6], refs[7:13], refs[13]
    state, occ, up, low, bath, damp = held
    copies = [
        pltpu.make_async_copy(src, dst, sems.at[index]) for index, (src, dst) in enumerate(zip(inputs, held))
    ]
    for copy in copies:
        copy.start()
    for copy in copies:
        copy.wait()
    _, half, slot, _ = start_of(lax.axis_index("aux"))
    problem = slot ^ half ^ 1 ^ which
    re, im = state[0, 0], state[0, 1]
    size = re.shape[0]

    @pl.when(problem == 0)
    def _():
        out[0:size] = 0.5 * ((re + im) + (re - im).T)

    @pl.when(problem == 1)
    def _():
        out[0:size] = 0.5 * ((re + im).T - (re - im))

    lane = lax.broadcasted_iota(jnp.int32, (META, size), 1)
    modes = occ.shape[1]
    row = jnp.zeros((META, size), F32)
    for mode in range(modes):
        for place, table in enumerate((occ, up, low)):
            row = jnp.where(lane == place * modes + mode, table[0, mode].astype(F32), row)
        for place, value in enumerate((damp[mode], bath[0, mode], bath[1, mode])):
            row = jnp.where(lane == (3 + place) * modes + mode, value, row)
    out[size : size + META] = row


def prepare_kernel(h_static, drive_op, couple, h_a, h_b, h_c, q_out):
    h_re = (h_static[0] + h_static[0].T) * 0.5
    h_im = (h_static[1] - h_static[1].T) * 0.5
    v_re = (drive_op[0] + drive_op[0].T) * 0.5
    v_im = (drive_op[1] - drive_op[1].T) * 0.5
    for h_out, moment in ((h_a, 0.0), (h_b, time_step / 2), (h_c, time_step)):
        drive = drive_amp * math.cos(drive_freq * moment)
        store_stack(h_out, 0, h_re + drive * v_re, h_im + drive * v_im)
    for mode in range(couple.shape[0]):
        q_out[mode] = (couple[mode] + couple[mode].T) * 0.5


def arrive_kernel(which, array, q_ref, h_ref, *refs):
    weights, base, rate, early = refs[-4:]
    problem, block, pair = role("aux")
    part = problem ^ 1 ^ which
    size = q_ref.shape[1]
    modes = q_ref.shape[0]
    meta = array[size : size + 1]

    def entry(place, mode):
        column = place * modes + mode
        return meta[:, column : column + 1]

    def constant(place, mode):
        return entry(3 + place, mode)

    total = jnp.zeros((1, 1), F32)
    for mode in range(modes):
        total = total + entry(0, mode) * constant(0, mode)
    rate[part] = jnp.broadcast_to(total, rate.shape[1:])
    value = array[0:size]
    base[part] = value
    m, p = products(h_ref.at[0], forms(value, True))
    early[part] = m - total * value + p.T

    near = 4 * block + 3 * pair
    inward = 1 - 2 * pair
    from_below = pair == 0
    sources = (
        jnp.where(part == 0, near + inward, near),
        near - inward,
        jnp.where(part == 0, near - 2 * inward, near + 2 * inward),
        jnp.where(part == 0, near + 2 * inward, near + 3 * inward),
    )
    link_kinds = (1 - part, 2 - part)
    partner_kinds = (2 * part, 3)
    link_sources = (jnp.where(part == 0, sources[1], sources[0]), jnp.where(part == 0, sources[2], sources[1]))
    partner_sources = (jnp.where(part == 0, sources[0], sources[2]), sources[3])

    def marked(place, source, mode):
        return entry(place, mode) == jnp.where(source < 0, -9, source).astype(F32)

    for index in range(2):
        kind = jnp.where(from_below, link_kinds[index], partner_kinds[index])
        source = jnp.where(from_below, link_sources[index], partner_sources[index])
        factors = []
        for mode in range(modes):
            down = jnp.where(marked(2, source, mode), entry(0, mode), 0.0)
            factors.append((down * constant(1, mode), down * constant(2, mode)))
        for row in range(0, size, CHUNK):
            w_re = sum(factors[mode][0] * q_ref[mode, row : row + CHUNK] for mode in range(modes))
            w_im = sum(factors[mode][1] * q_ref[mode, row : row + CHUNK] for mode in range(modes))
            store_rows(weights, 4 * part + kind, row, size, (w_re, w_im, w_re + w_im))
    for index in range(2):
        kind = jnp.where(from_below, partner_kinds[index], link_kinds[index])
        source = jnp.where(from_below, partner_sources[index], link_sources[index])
        factors = [jnp.where(marked(1, source, mode), 1.0, 0.0) for mode in range(modes)]
        for row in range(0, size, CHUNK):
            w_re = sum(factors[mode] * q_ref[mode, row : row + CHUNK] for mode in range(modes))
            store_rows(weights, 4 * part + kind, row, size, (w_re,))


N_OWN, N_LINK_N, N_LINK_F, N_PARTNER_F, F_OWN, F_LINK_N, F_PARTNER_F, F_PARTNER_N = range(8)


def term(weights, row, source):
    m, p = products(weights.at[row], source)
    return m + p.T


def cross_kernel(base, weights, early, near_out, far_out):
    _, _, pair = role("aux")

    def body(lower):
        near_out[...] = early[0] + term(weights, N_OWN, forms(base[1], lower))
        far_out[...] = early[1] + term(weights, F_OWN, forms(base[0], not lower))

    by_type(pair == 1, body)


def own_kernel(near, far, h_ref, weights, rate, near_out, far_out):
    _, _, pair = role("aux")
    x_n, x_f = near[...], far[...]
    f_n, f_f = forms(x_n, True), forms(x_f, True)
    m_n, p_n = products(h_ref.at[0], f_n)
    m_f, p_f = products(h_ref.at[0], f_f)
    m_n = m_n - rate[0][0:1, 0:1] * x_n
    m_f = m_f - rate[1][0:1, 0:1] * x_f

    def body(lower):
        m_nf, p_nf = products(weights.at[N_OWN], f_f if lower else f_f[:1])
        m_fn, p_fn = products(weights.at[F_OWN], f_n[:1] if lower else f_n)
        near_out[...] = m_n + m_nf + (p_n + p_nf).T
        far_out[...] = m_f + m_fn + (p_f + p_fn).T

    by_type(pair == 1, body)


def pick(one, two, sorted_already):
    if sorted_already:
        return one[...], two[...]
    problem, _, _ = role("aux")
    size = one.shape[1]
    near_first = problem == 1
    one, two = one[0:size], two[0:size]
    return jnp.where(near_first, one, two), jnp.where(near_first, two, one)


def partner_kernel(sorted_already, one, two, weights, near, far, near_out, far_out):
    _, _, pair = role("aux")
    x_n, x_f = pick(one, two, sorted_already)

    def body(lower):
        f_n, f_f = forms(x_n, lower), forms(x_f, lower)
        near_out[...] = near[...] + term(weights, N_PARTNER_F, f_f)
        m_a, p_a = products(weights.at[F_PARTNER_F], f_f)
        m_b, p_b = products(weights.at[F_PARTNER_N], f_n)
        far_out[...] = far[...] + m_a + m_b + (p_a + p_b).T

    by_type(pair == 1, body)


def part_kernel(row, source, weights, early, out):
    _, _, pair = role("aux")

    def body(lower):
        out[...] = early[...] + term(weights, row, forms(source[...], lower))

    by_type(pair == 0, body)


def finish_kernel(row, part, step, weight, source, weights, early, base, acc, out, acc_out):
    _, _, pair = role("aux")

    def body(lower):
        slope = early[...] + term(weights, row, forms(source[...], lower))
        out[...] = base[part] + step * slope
        acc_out[...] = (acc[part] if len(acc.shape) == 3 else acc[...]) + weight * slope

    by_type(pair == 0, body)


def sent_far(which):
    problem, _, _ = role("aux")
    return problem ^ 1 ^ which


def first_part_kernel(array, weights, near, far, near_out, far_out):
    _, _, pair = role("aux")
    is_far = sent_far(0)

    def body(lower):
        source = forms(array[0 : array.shape[1]], lower)
        near_out[...] = near[...] + term(weights, N_LINK_N + is_far, source)

        @pl.when(is_far == 0)
        def _():
            far_out[...] = far[...] + term(weights, F_LINK_N, source)

        @pl.when(is_far == 1)
        def _():
            far_out[...] = far[...]

    by_type(pair == 0, body)


def first_near_kernel(step, weight, array, weights, early, base, out, acc_out):
    _, _, pair = role("aux")

    def body(lower):
        source = forms(array[0 : array.shape[1]], lower)
        slope = early[...] + term(weights, N_LINK_N + sent_far(1), source)
        out[...] = base[0] + step * slope
        acc_out[...] = base[0] + weight * slope

    by_type(pair == 0, body)


def first_far_kernel(step, weight, array, weights, early, base, out, acc_out):
    _, _, pair = role("aux")
    is_far = sent_far(1)

    def store(slope):
        out[...] = base[1] + step * slope
        acc_out[...] = base[1] + weight * slope

    def body(lower):
        @pl.when(is_far == 0)
        def _():
            store(early[...] + term(weights, F_LINK_N, forms(array[0 : array.shape[1]], lower)))

    by_type(pair == 0, body)

    @pl.when(is_far == 1)
    def _():
        store(early[...])


def last_far_kernel(weight, source, weights, early, acc, out):
    _, _, pair = role("aux")

    def body(lower):
        out[...] = acc[...] + weight * (early[...] + term(weights, F_LINK_N, forms(source[...], lower)))

    by_type(pair == 0, body)


def last_near_kernel(weight, source, weights, early, acc, far, first, second):
    problem, _, pair = role("aux")
    near_first = pair == problem

    def body(lower):
        near = acc[...] + weight * (early[...] + term(weights, N_LINK_F, forms(source[...], lower)))
        first[...] = jnp.where(near_first, near, far[...])
        second[...] = jnp.where(near_first, far[...], near)

    by_type(pair == 0, body)


def restore_kernel(first, second, first_sent, second_sent, out_hbm, out, sems):
    device = lax.axis_index("aux")
    slot = device & 1
    keep_first, keep_second = kept(device)
    one = jnp.where(keep_first, first_sent[...], first[...])
    two = jnp.where(keep_second, second_sent[...], second[...])
    herm = jnp.where(slot == 0, one, two)
    anti = jnp.where(slot == 0, two, one)
    total = herm + anti.T
    diff = herm.T - anti
    copies = []
    for half, value in enumerate((total + diff, total - diff)):
        out[0, half] = 0.5 * value
        copies.append(pltpu.make_async_copy(out.at[0, half], out_hbm.at[0, half], sems.at[half]))
        copies[-1].start()
    for copy in copies:
        copy.wait()


def call(kernel, out_shapes, args, smem=(), flops=0, space=None, scratch=(), grant=32, aliases=None, out_space=None):
    shapes = [jax.ShapeDtypeStruct(shape, dtype) for shape, dtype in out_shapes]
    moved = sum(math.prod(a.shape) * a.dtype.itemsize for a in list(args) + shapes)
    single = len(shapes) == 1
    return pl.pallas_call(
        kernel,
        out_shape=shapes[0] if single else shapes,
        in_specs=[space or (SMEM if index in smem else VMEM) for index in range(len(args))],
        out_specs=(out_space or VMEM) if single else [VMEM] * len(shapes),
        scratch_shapes=scratch,
        input_output_aliases=aliases or {},
        cost_estimate=pl.CostEstimate(flops=flops, bytes_accessed=moved, transcendentals=0),
        compiler_params=pltpu.CompilerParams(vmem_limit_bytes=grant * 1024 * 1024),
    )(*args)


def on_device(state, h_static, drive_op, couple, bath_coef, damping, occupation, raise_nbr, lower_nbr):
    count = lax.axis_size("aux")
    size = state.shape[-1]
    modes = couple.shape[0]
    first_to, rows_to, columns_to, link_to, core_to, back_to = permutations(count)
    pair_shape = (2, size, size)
    unit = 2 * size**3

    def send(value, pairs):
        return lax.ppermute(value, "aux", pairs)

    tall = ((size + META, size), F32)
    tables = [occupation, raise_nbr, lower_nbr, bath_coef, damping]
    first, second = (
        call(
            partial(convert_kernel, which),
            [tall],
            [state] + tables,
            space=pl.BlockSpec(memory_space=pltpu.HBM),
            grant=60,
            scratch=[pltpu.VMEM(state.shape, F32)]
            + [pltpu.SMEM(table.shape, table.dtype) for table in tables]
            + [pltpu.SemaphoreType.DMA((1 + len(tables),))],
        )
        for which in range(2)
    )
    device = lax.axis_index("aux")
    _, _, slot, parity = start_of(device)
    keep_first = targets_of(device)[0] == device
    crossed = send(second, rows_to)
    first = jnp.where(keep_first, first, send(first, first_to))
    is_straight = straight(device)
    turned = send(jnp.where(is_straight, crossed, second), columns_to)
    second = jnp.where(slot == parity, jnp.where(is_straight, second, crossed), turned)
    *h_now, q_all = call(
        prepare_kernel, [((1, 6 * size, size), BF16)] * 3 + [((modes, size, size), F32)], [h_static, drive_op, couple]
    )
    flat = ((size, size), F32)

    held = [((8, 6 * size, size), BF16), (pair_shape, F32), ((2, 8, 128), F32), (pair_shape, F32)]
    state_now = call(partial(arrive_kernel, 0), held, [first, q_all, h_now[0]], flops=9 * unit)
    link = [send(first, link_to)]
    partner = [send(first, core_to)]
    weights, base, rate, early = call(
        partial(arrive_kernel, 1),
        held,
        [second, q_all, h_now[0], *state_now],
        flops=9 * unit,
        aliases={3 + index: index for index in range(4)},
    )
    link.append(send(second, link_to))
    partner.append(send(second, core_to))
    near_e, far_e = call(cross_kernel, [flat, flat], [base, weights, early], flops=15 * unit)
    steps = (time_step / 2, time_step / 2, time_step)
    shares = (time_step / 6, time_step / 3, time_step / 3, time_step / 6)

    def with_partner(stage, near_e, far_e):
        return call(
            partial(partner_kernel, stage > 0), [flat, flat], [*partner, weights, near_e, far_e], flops=27 * unit
        )

    def own(stage, near, far):
        args = [near, far, h_now[(0, 1, 1, 2)[stage]], weights, rate]
        return call(own_kernel, [flat, flat], args, flops=33 * unit)

    def part(row, source, early):
        return call(partial(part_kernel, row), [flat], [source, weights, early], flops=9 * unit)

    def finish(stage, row, which, source, early, acc):
        return call(
            partial(finish_kernel, row, which, steps[stage], shares[stage]),
            [flat, flat],
            [source, weights, early, base, acc],
            flops=9 * unit,
        )

    near_e, far_e = with_partner(0, near_e, far_e)
    near_e, far_e = call(first_part_kernel, [flat, flat], [link[0], weights, near_e, far_e], flops=18 * unit)
    near, near_acc = call(
        partial(first_near_kernel, steps[0], shares[0]), [flat, flat], [link[1], weights, near_e, base], flops=9 * unit
    )
    far, far_acc = call(
        partial(first_far_kernel, steps[0], shares[0]), [flat, flat], [link[1], weights, far_e, base], flops=9 * unit
    )
    link_n, link_f = send(near, link_to), send(far, link_to)
    partner = [send(near, core_to), send(far, core_to)]
    near_e, far_e = with_partner(1, *own(1, near, far))
    far, far_acc = finish(1, F_LINK_N, 1, link_n, far_e, far_acc)
    next_f = send(far, link_to)
    near_e = part(N_LINK_N, link_n, near_e)
    near, near_acc = finish(1, N_LINK_F, 0, link_f, near_e, near_acc)
    link_n, link_f = send(near, link_to), next_f
    partner = [send(near, core_to), send(far, core_to)]
    near_e, far_e = with_partner(2, *own(2, near, far))
    near_e = part(N_LINK_F, link_f, near_e)
    near, near_acc = finish(2, N_LINK_N, 0, link_n, near_e, near_acc)
    far, far_acc = finish(2, F_LINK_N, 1, link_n, far_e, far_acc)
    link_n, link_f = send(near, link_to), send(far, link_to)
    partner = [send(near, core_to), send(far, core_to)]
    near_e, far_e = with_partner(3, *own(3, near, far))
    far = call(partial(last_far_kernel, shares[3]), [flat], [link_n, weights, far_e, far_acc], flops=9 * unit)
    near_e = part(N_LINK_N, link_n, near_e)
    first, second = call(
        partial(last_near_kernel, shares[3]), [flat, flat], [link_f, weights, near_e, near_acc, far], flops=9 * unit
    )
    back = [send(first, back_to[0]), send(second, back_to[1]), first, second]
    return call(
        restore_kernel,
        [(state.shape, F32)],
        back,
        out_space=pl.BlockSpec(memory_space=pltpu.HBM),
        scratch=[pltpu.VMEM(state.shape, F32), pltpu.SemaphoreType.DMA((2,))],
    )


def solution(mesh):
    return jax.shard_map(
        on_device,
        mesh=mesh,
        in_specs=(
            P("aux", None, None, None),
            P(),
            P(),
            P(),
            P(),
            P(),
            P("aux", None),
            P("aux", None),
            P("aux", None),
        ),
        out_specs=P("aux", None, None, None),
        check_vma=False,
    )
```

```python
import math
from functools import partial

import jax
import jax.numpy as jnp
from jax import lax
from jax.experimental import pallas as pl
from jax.experimental.pallas import tpu as pltpu
from jax.sharding import PartitionSpec as P


time_step = 0.05
drive_amp = 2.0
drive_freq = 20.0
META = 8
CHUNK = 32
F32 = jnp.float32
BF16 = jnp.bfloat16
VMEM = pl.BlockSpec(memory_space=pltpu.VMEM)
SMEM = pl.BlockSpec(memory_space=pltpu.SMEM)


def chip_of(problem, block):
    group, odd = block >> 1, block & 1
    return group * 4 + problem * 2 + (odd ^ (group & 1))


def device_of(problem, block, pair):
    return chip_of(problem, block) * 2 + ((block & 1) ^ pair)


def role_of(device):
    core, x, problem, group = device & 1, (device >> 1) & 1, (device >> 2) & 1, device >> 3
    odd = x ^ (group & 1)
    return problem, 2 * group + odd, core ^ odd


def permutations(count):
    blocks = count // 4
    first, second, link = [], [], []
    for device in range(count):
        block, half, slot = device >> 2, (device >> 1) & 1, device & 1
        first.append((device, device_of(slot, block, half)))
        second.append((device, device_of(1 - slot, block, half)))
    for problem in range(2):
        for block in range(blocks - 1):
            here, there = device_of(problem, block, 1), device_of(problem, block + 1, 0)
            link += [(here, there), (there, here)]
    for block, pair in ((0, 0), (blocks - 1, 1)):
        here, there = device_of(0, block, pair), device_of(1, block, pair)
        link += [(here, there), (there, here)]
    core = [(device, device ^ 1) for device in range(count)]
    return full(first), full(second), sorted(link), core


def full(pairs):
    fixed = [a for a, b in pairs if a == b]
    swaps = {}
    for place in range(0, len(fixed) - 3, 4):
        for a, b in ((fixed[place], fixed[place + 2]), (fixed[place + 1], fixed[place + 3])):
            swaps.update({a: b, b: a})
    return [(a, swaps.get(a, b)) for a, b in pairs]


def kept(device):
    block, half, slot = device >> 2, (device >> 1) & 1, device & 1
    return device_of(slot, block, half) == device, device_of(1 - slot, block, half) == device


def flipped(pairs):
    return sorted((b, a) for a, b in pairs)


def split(value):
    high = value.astype(BF16)
    return high, (value - high.astype(F32)).astype(BF16)


def store_stack(ref, index, w_re, w_im=None):
    size = w_re.shape[0]
    for place, value in enumerate((w_re,) if w_im is None else (w_re, w_im, w_re + w_im)):
        high, low = split(value)
        ref[index, 2 * place * size : (2 * place + 1) * size] = high
        ref[index, (2 * place + 1) * size : (2 * place + 2) * size] = low


def store_rows(ref, index, row, size, values):
    for place, value in enumerate(values):
        high, low = split(value)
        start = 2 * place * size + row
        ref[index, start : start + value.shape[0]] = high
        ref[index, start + size : start + size + value.shape[0]] = low


def dot_nn(a, b):
    return lax.dot_general(a, b, (((1,), (0,)), ((), ())), preferred_element_type=F32)


def dot_nt(a, b):
    return lax.dot_general(a, b, (((1,), (1,)), ((), ())), preferred_element_type=F32)


def three(stack, place, source, dot):
    high, low = source
    size = high.shape[0]
    both = stack[2 * place * size : (2 * place + 2) * size]
    wide = dot(both, high)
    return wide[:size] + wide[size:] + dot(both[:size], low)


def forms(source, full):
    if not full:
        return (split(source),)
    turned = source.T
    return split(source), split(source + turned), split(source - turned)


def products(stack, source):
    if len(source) == 1:
        return -three(stack, 0, source[0], dot_nt), three(stack, 0, source[0], dot_nn)
    shared = three(stack, 2, source[0], dot_nn)
    return shared - three(stack, 0, source[1], dot_nn), shared - three(stack, 1, source[2], dot_nn)


def role(axis):
    return role_of(lax.axis_index(axis))


def by_type(lower, body):
    @pl.when(lower)
    def _():
        body(True)

    @pl.when(jnp.logical_not(lower))
    def _():
        body(False)


def convert_kernel(which, state_hbm, occ_hbm, up_hbm, low_hbm, out, state, occ, up, low, sems):
    copies = [
        pltpu.make_async_copy(src, dst, sems.at[index])
        for index, (src, dst) in enumerate(((state_hbm, state), (occ_hbm, occ), (up_hbm, up), (low_hbm, low)))
    ]
    for copy in copies:
        copy.start()
    copies[0].wait()
    slot = lax.axis_index("aux") & 1
    re, im = state[0, 0], state[0, 1]
    size = re.shape[0]

    @pl.when(slot == which)
    def _():
        out[0:size] = 0.5 * ((re + im) + (re - im).T)

    @pl.when(slot != which)
    def _():
        out[0:size] = 0.5 * ((re + im).T - (re - im))

    for copy in copies[1:]:
        copy.wait()
    lane = lax.broadcasted_iota(jnp.int32, (META, size), 1)
    modes = occ.shape[1]
    row = jnp.zeros((META, size), F32)
    for mode in range(modes):
        for place, table in enumerate((occ, up, low)):
            row = jnp.where(lane == place * modes + mode, table[0, mode].astype(F32), row)
    out[size : size + META] = row


def prepare_kernel(h_static, drive_op, couple, bath_coef, damping, h_a, h_b, h_c, q_out, damp_out):
    h_re = (h_static[0] + h_static[0].T) * 0.5
    h_im = (h_static[1] - h_static[1].T) * 0.5
    v_re = (drive_op[0] + drive_op[0].T) * 0.5
    v_im = (drive_op[1] - drive_op[1].T) * 0.5
    for h_out, moment in ((h_a, 0.0), (h_b, time_step / 2), (h_c, time_step)):
        drive = drive_amp * math.cos(drive_freq * moment)
        store_stack(h_out, 0, h_re + drive * v_re, h_im + drive * v_im)
    for mode in range(couple.shape[0]):
        q_out[mode] = (couple[mode] + couple[mode].T) * 0.5
        for place, value in enumerate((damping[mode], bath_coef[0, mode], bath_coef[1, mode])):
            damp_out[3 * mode + place] = jnp.full(damp_out.shape[1:], value, F32)


def arrive_kernel(which, array, q_ref, damp, h_ref, *refs):
    weights, base, rate, early = refs[-4:]
    problem, block, pair = role("aux")
    part = pair ^ problem ^ which
    size = q_ref.shape[1]
    modes = q_ref.shape[0]
    meta = array[size : size + 1]

    def entry(place, mode):
        column = place * modes + mode
        return meta[:, column : column + 1]

    def constant(place, mode):
        return damp[3 * mode + place][0:1, 0:1]

    total = jnp.zeros((1, 1), F32)
    for mode in range(modes):
        total = total + entry(0, mode) * constant(0, mode)
    rate[part] = jnp.broadcast_to(total, rate.shape[1:])
    value = array[0:size]
    base[part] = value
    m, p = products(h_ref.at[0], forms(value, True))
    early[part] = m - total * value + p.T

    near = 4 * block + 3 * pair
    inward = 1 - 2 * pair
    from_below = pair == 0
    sources = (
        jnp.where(part == 0, near + inward, near),
        near - inward,
        jnp.where(part == 0, near - 2 * inward, near + 2 * inward),
        jnp.where(part == 0, near + 2 * inward, near + 3 * inward),
    )
    link_kinds = (1 - part, 2 - part)
    partner_kinds = (2 * part, 3)
    link_sources = (jnp.where(part == 0, sources[1], sources[0]), jnp.where(part == 0, sources[2], sources[1]))
    partner_sources = (jnp.where(part == 0, sources[0], sources[2]), sources[3])

    def marked(place, source, mode):
        return entry(place, mode) == jnp.where(source < 0, -9, source).astype(F32)

    for index in range(2):
        kind = jnp.where(from_below, link_kinds[index], partner_kinds[index])
        source = jnp.where(from_below, link_sources[index], partner_sources[index])
        factors = []
        for mode in range(modes):
            down = jnp.where(marked(2, source, mode), entry(0, mode), 0.0)
            factors.append((down * constant(1, mode), down * constant(2, mode)))
        for row in range(0, size, CHUNK):
            w_re = sum(factors[mode][0] * q_ref[mode, row : row + CHUNK] for mode in range(modes))
            w_im = sum(factors[mode][1] * q_ref[mode, row : row + CHUNK] for mode in range(modes))
            store_rows(weights, 4 * part + kind, row, size, (w_re, w_im, w_re + w_im))
    for index in range(2):
        kind = jnp.where(from_below, partner_kinds[index], link_kinds[index])
        source = jnp.where(from_below, partner_sources[index], link_sources[index])
        factors = [jnp.where(marked(1, source, mode), 1.0, 0.0) for mode in range(modes)]
        for row in range(0, size, CHUNK):
            w_re = sum(factors[mode] * q_ref[mode, row : row + CHUNK] for mode in range(modes))
            store_rows(weights, 4 * part + kind, row, size, (w_re,))


N_OWN, N_LINK_N, N_LINK_F, N_PARTNER_F, F_OWN, F_LINK_N, F_PARTNER_F, F_PARTNER_N = range(8)


def term(weights, row, source):
    m, p = products(weights.at[row], source)
    return m + p.T


def cross_kernel(base, weights, early, near_out, far_out):
    _, _, pair = role("aux")

    def body(lower):
        near_out[...] = early[0] + term(weights, N_OWN, forms(base[1], lower))
        far_out[...] = early[1] + term(weights, F_OWN, forms(base[0], not lower))

    by_type(pair == 1, body)


def own_kernel(near, far, h_ref, weights, rate, near_out, far_out):
    _, _, pair = role("aux")
    x_n, x_f = near[...], far[...]
    f_n, f_f = forms(x_n, True), forms(x_f, True)
    m_n, p_n = products(h_ref.at[0], f_n)
    m_f, p_f = products(h_ref.at[0], f_f)
    m_n = m_n - rate[0][0:1, 0:1] * x_n
    m_f = m_f - rate[1][0:1, 0:1] * x_f

    def body(lower):
        m_nf, p_nf = products(weights.at[N_OWN], f_f if lower else f_f[:1])
        m_fn, p_fn = products(weights.at[F_OWN], f_n[:1] if lower else f_n)
        near_out[...] = m_n + m_nf + (p_n + p_nf).T
        far_out[...] = m_f + m_fn + (p_f + p_fn).T

    by_type(pair == 1, body)


def pick(one, two, pair, sorted_already):
    if sorted_already:
        return one[...], two[...]
    problem, _, _ = role("aux")
    size = one.shape[1]
    near_first = pair == problem
    one, two = one[0:size], two[0:size]
    return jnp.where(near_first, one, two), jnp.where(near_first, two, one)


def partner_kernel(sorted_already, one, two, weights, near, far, near_out, far_out):
    _, _, pair = role("aux")
    x_n, x_f = pick(one, two, 1 - pair, sorted_already)

    def body(lower):
        f_n, f_f = forms(x_n, lower), forms(x_f, lower)
        near_out[...] = near[...] + term(weights, N_PARTNER_F, f_f)
        m_a, p_a = products(weights.at[F_PARTNER_F], f_f)
        m_b, p_b = products(weights.at[F_PARTNER_N], f_n)
        far_out[...] = far[...] + m_a + m_b + (p_a + p_b).T

    by_type(pair == 1, body)


def part_kernel(row, source, weights, early, out):
    _, _, pair = role("aux")

    def body(lower):
        out[...] = early[...] + term(weights, row, forms(source[...], lower))

    by_type(pair == 0, body)


def finish_kernel(row, part, step, weight, source, weights, early, base, acc, out, acc_out):
    _, _, pair = role("aux")

    def body(lower):
        slope = early[...] + term(weights, row, forms(source[...], lower))
        out[...] = base[part] + step * slope
        acc_out[...] = (acc[part] if len(acc.shape) == 3 else acc[...]) + weight * slope

    by_type(pair == 0, body)


def sent_far(which):
    problem, _, pair = role("aux")
    return pair ^ 1 ^ problem ^ which


def first_part_kernel(array, weights, near, far, near_out, far_out):
    _, _, pair = role("aux")
    is_far = sent_far(0)

    def body(lower):
        source = forms(array[0 : array.shape[1]], lower)
        near_out[...] = near[...] + term(weights, N_LINK_N + is_far, source)

        @pl.when(is_far == 0)
        def _():
            far_out[...] = far[...] + term(weights, F_LINK_N, source)

        @pl.when(is_far == 1)
        def _():
            far_out[...] = far[...]

    by_type(pair == 0, body)


def first_near_kernel(step, weight, array, weights, early, base, out, acc_out):
    _, _, pair = role("aux")

    def body(lower):
        source = forms(array[0 : array.shape[1]], lower)
        slope = early[...] + term(weights, N_LINK_N + sent_far(1), source)
        out[...] = base[0] + step * slope
        acc_out[...] = base[0] + weight * slope

    by_type(pair == 0, body)


def first_far_kernel(step, weight, array, weights, early, base, out, acc_out):
    _, _, pair = role("aux")
    is_far = sent_far(1)

    def store(slope):
        out[...] = base[1] + step * slope
        acc_out[...] = base[1] + weight * slope

    def body(lower):
        @pl.when(is_far == 0)
        def _():
            store(early[...] + term(weights, F_LINK_N, forms(array[0 : array.shape[1]], lower)))

    by_type(pair == 0, body)

    @pl.when(is_far == 1)
    def _():
        store(early[...])


def last_far_kernel(weight, source, weights, early, acc, out):
    _, _, pair = role("aux")

    def body(lower):
        out[...] = acc[...] + weight * (early[...] + term(weights, F_LINK_N, forms(source[...], lower)))

    by_type(pair == 0, body)


def last_near_kernel(weight, source, weights, early, acc, far, first, second):
    problem, _, pair = role("aux")
    near_first = pair == problem

    def body(lower):
        near = acc[...] + weight * (early[...] + term(weights, N_LINK_F, forms(source[...], lower)))
        first[...] = jnp.where(near_first, near, far[...])
        second[...] = jnp.where(near_first, far[...], near)

    by_type(pair == 0, body)


def restore_kernel(first, second, first_sent, second_sent, out_hbm, out, sems):
    device = lax.axis_index("aux")
    slot = device & 1
    keep_first, keep_second = kept(device)
    one = jnp.where(keep_first, first_sent[...], first[...])
    two = jnp.where(keep_second, second_sent[...], second[...])
    herm = jnp.where(slot == 0, one, two)
    anti = jnp.where(slot == 0, two, one)
    total = herm + anti.T
    diff = herm.T - anti
    copies = []
    for half, value in enumerate((total + diff, total - diff)):
        out[0, half] = 0.5 * value
        copies.append(pltpu.make_async_copy(out.at[0, half], out_hbm.at[0, half], sems.at[half]))
        copies[-1].start()
    for copy in copies:
        copy.wait()


def call(kernel, out_shapes, args, smem=(), flops=0, space=None, scratch=(), grant=32, aliases=None, out_space=None):
    shapes = [jax.ShapeDtypeStruct(shape, dtype) for shape, dtype in out_shapes]
    moved = sum(math.prod(a.shape) * a.dtype.itemsize for a in list(args) + shapes)
    single = len(shapes) == 1
    return pl.pallas_call(
        kernel,
        out_shape=shapes[0] if single else shapes,
        in_specs=[space or (SMEM if index in smem else VMEM) for index in range(len(args))],
        out_specs=(out_space or VMEM) if single else [VMEM] * len(shapes),
        scratch_shapes=scratch,
        input_output_aliases=aliases or {},
        cost_estimate=pl.CostEstimate(flops=flops, bytes_accessed=moved, transcendentals=0),
        compiler_params=pltpu.CompilerParams(vmem_limit_bytes=grant * 1024 * 1024),
    )(*args)


def on_device(state, h_static, drive_op, couple, bath_coef, damping, occupation, raise_nbr, lower_nbr):
    count = lax.axis_size("aux")
    size = state.shape[-1]
    modes = couple.shape[0]
    first_to, second_to, link_to, core_to = permutations(count)
    pair_shape = (2, size, size)
    unit = 2 * size**3

    def send(value, pairs):
        return lax.ppermute(value, "aux", pairs)

    tall = ((size + META, size), F32)
    tables = [occupation, raise_nbr, lower_nbr]
    first, second = (
        call(
            partial(convert_kernel, which),
            [tall],
            [state] + tables,
            space=pl.BlockSpec(memory_space=pltpu.HBM),
            grant=60,
            scratch=[pltpu.VMEM(state.shape, F32)]
            + [pltpu.SMEM(table.shape, jnp.int32) for table in tables]
            + [pltpu.SemaphoreType.DMA((4,))],
        )
        for which in range(2)
    )
    keep_first, keep_second = kept(lax.axis_index("aux"))
    first = jnp.where(keep_first, first, send(first, first_to))
    second = jnp.where(keep_second, second, send(second, second_to))
    *h_now, q_all, damp = call(
        prepare_kernel,
        [((1, 6 * size, size), BF16)] * 3 + [((modes, size, size), F32), ((3 * modes, 8, 128), F32)],
        [h_static, drive_op, couple, bath_coef, damping],
        smem=(3, 4),
    )
    flat = ((size, size), F32)

    held = [((8, 6 * size, size), BF16), (pair_shape, F32), ((2, 8, 128), F32), (pair_shape, F32)]
    state_now = call(partial(arrive_kernel, 0), held, [first, q_all, damp, h_now[0]], flops=9 * unit)
    link = [send(first, link_to)]
    partner = [send(first, core_to)]
    weights, base, rate, early = call(
        partial(arrive_kernel, 1),
        held,
        [second, q_all, damp, h_now[0], *state_now],
        flops=9 * unit,
        aliases={4 + index: index for index in range(4)},
    )
    link.append(send(second, link_to))
    partner.append(send(second, core_to))
    near_e, far_e = call(cross_kernel, [flat, flat], [base, weights, early], flops=15 * unit)
    steps = (time_step / 2, time_step / 2, time_step)
    shares = (time_step / 6, time_step / 3, time_step / 3, time_step / 6)

    def with_partner(stage, near_e, far_e):
        return call(
            partial(partner_kernel, stage > 0), [flat, flat], [*partner, weights, near_e, far_e], flops=27 * unit
        )

    def own(stage, near, far):
        args = [near, far, h_now[(0, 1, 1, 2)[stage]], weights, rate]
        return call(own_kernel, [flat, flat], args, flops=33 * unit)

    def part(row, source, early):
        return call(partial(part_kernel, row), [flat], [source, weights, early], flops=9 * unit)

    def finish(stage, row, which, source, early, acc):
        return call(
            partial(finish_kernel, row, which, steps[stage], shares[stage]),
            [flat, flat],
            [source, weights, early, base, acc],
            flops=9 * unit,
        )

    near_e, far_e = with_partner(0, near_e, far_e)
    near_e, far_e = call(first_part_kernel, [flat, flat], [link[0], weights, near_e, far_e], flops=18 * unit)
    near, near_acc = call(
        partial(first_near_kernel, steps[0], shares[0]), [flat, flat], [link[1], weights, near_e, base], flops=9 * unit
    )
    far, far_acc = call(
        partial(first_far_kernel, steps[0], shares[0]), [flat, flat], [link[1], weights, far_e, base], flops=9 * unit
    )
    link_n, link_f = send(near, link_to), send(far, link_to)
    partner = [send(near, core_to), send(far, core_to)]
    near_e, far_e = with_partner(1, *own(1, near, far))
    far, far_acc = finish(1, F_LINK_N, 1, link_n, far_e, far_acc)
    next_f = send(far, link_to)
    near_e = part(N_LINK_N, link_n, near_e)
    near, near_acc = finish(1, N_LINK_F, 0, link_f, near_e, near_acc)
    link_n, link_f = send(near, link_to), next_f
    partner = [send(near, core_to), send(far, core_to)]
    near_e, far_e = with_partner(2, *own(2, near, far))
    near_e = part(N_LINK_F, link_f, near_e)
    near, near_acc = finish(2, N_LINK_N, 0, link_n, near_e, near_acc)
    far, far_acc = finish(2, F_LINK_N, 1, link_n, far_e, far_acc)
    link_n, link_f = send(near, link_to), send(far, link_to)
    partner = [send(near, core_to), send(far, core_to)]
    near_e, far_e = with_partner(3, *own(3, near, far))
    far = call(partial(last_far_kernel, shares[3]), [flat], [link_n, weights, far_e, far_acc], flops=9 * unit)
    near_e = part(N_LINK_N, link_n, near_e)
    first, second = call(
        partial(last_near_kernel, shares[3]), [flat, flat], [link_f, weights, near_e, near_acc, far], flops=9 * unit
    )
    back = [send(first, flipped(first_to)), send(second, flipped(second_to)), first, second]
    return call(
        restore_kernel,
        [(state.shape, F32)],
        back,
        out_space=pl.BlockSpec(memory_space=pltpu.HBM),
        scratch=[pltpu.VMEM(state.shape, F32), pltpu.SemaphoreType.DMA((2,))],
    )


def solution(mesh):
    return jax.shard_map(
        on_device,
        mesh=mesh,
        in_specs=(
            P("aux", None, None, None),
            P(),
            P(),
            P(),
            P(),
            P(),
            P("aux", None),
            P("aux", None),
            P("aux", None),
        ),
        out_specs=P("aux", None, None, None),
        check_vma=False,
    )
```
